256 devices in a mesh: tm: 4 (over x), height: 4 (over y), width: 16 (over z, core).
Axes of the slice: x: 4, y: 4, z: 8, core: 2. Of those that a mesh axis runs over, the one named last changes fastest.
Arguments:
- video: bfloat16 [64, 64, 256, 256], P('tm', 'height', 'width'), may hold values from -12 to 12
- w_space: bfloat16 [3, 3, 256, 256], replicated, may hold values from -0.125 to 0.125
- w_time: bfloat16 [3, 256, 256], replicated, may hold values from -0.21875 to 0.21875
- norm_gain: float32 [256], replicated, may hold values from 0.1 to 1.9
- norm_bias: float32 [256], replicated, may hold values from -1 to 1
- w_qkv: bfloat16 [256, 768], replicated, may hold values from -64 to 64
- w_out: bfloat16 [256, 256], replicated, may hold values from -0.375 to 0.375
Outputs:
- block_out: bfloat16 [64, 64, 256, 256], P('tm', 'height', 'width')
The draws below stay inside these ranges and needn't reach their ends.
All inputs are finite; a program needn't handle non-finite values.
Results may differ from the reference program's by a relative error of at most 0.012.
Values may be sent and summed in bfloat16 or wider, within the bound.
No kernel may reach another device: no remote copies, remote signals or barrier semaphores. Data moves between devices by JAX's collectives and lax.ppermute only.
A program may use at most 128 MiB of HBM per device.

```python
import math
import jax
import jax.numpy as jnp
from jax import lax

C = 256
HEADS = 8
GROUPS = 32
FRAMES = 64
HEIGHT = 64
WIDTH = 256


def draw_video(key, part):
    frame_pos = jnp.arange(FRAMES).astype(jnp.float32) / max(FRAMES - 1, 1)
    row_pos = jnp.arange(HEIGHT).astype(jnp.float32) / max(HEIGHT - 1, 1)
    col_pos = jnp.arange(WIDTH).astype(jnp.float32) / max(WIDTH - 1, 1)
    factor = jnp.sqrt((1.0 + 2.0 * frame_pos)[:, None, None] * (1.0 + 2.0 * row_pos)[None, :, None] * (1.0 + 2.0 * col_pos)[None, None, :])
    noise = jax.random.normal(jax.random.fold_in(key, 14), (FRAMES, HEIGHT, WIDTH, C), jnp.float32)
    return jnp.clip(noise * factor[:, :, :, None], -12.0, 12.0).astype(jnp.bfloat16)


def draw_w_qkv(key, part):
    base = jax.random.normal(jax.random.fold_in(key, 21), (C, 3 * C), jnp.float32) / jnp.sqrt(float(C))
    base = jnp.clip(base, -6.0 / jnp.sqrt(float(C)), 6.0 / jnp.sqrt(float(C)))
    return jnp.clip(base, -64.0, 64.0).astype(jnp.bfloat16)


def gaussian(rng, shape, deviation, limit, held_as=jnp.bfloat16):
    drawn = deviation * jax.random.normal(rng, shape, jnp.float32)
    return jnp.clip(drawn, min=-limit, max=limit).astype(held_as)


def setup_inputs(seed: int = 0) -> dict:
    seeds = jax.random.split(jax.random.key(seed), 8)
    return {
        "video": draw_video(jax.random.fold_in(seeds[7], 71), 0),
        "w_space": gaussian(seeds[1], (3, 3, C, C), (9 * C) ** -0.5, 0.125),
        "w_time": gaussian(seeds[2], (3, C, C), (3 * C) ** -0.5, 0.21875),
        "norm_gain": jnp.clip(1.0 + 0.18 * jax.random.normal(seeds[3], (C,), jnp.float32), 0.1, 1.9),
        "norm_bias": jnp.clip(jax.random.uniform(seeds[4], (C,), jnp.float32, -1.0, 1.0), -1.0, 1.0),
        "w_qkv": draw_w_qkv(jax.random.fold_in(seeds[7], 71), 0),
        "w_out": gaussian(seeds[6], (C, C), C ** -0.5, 0.375),
    }


def space_frame(frame, w_space):
    rows, cols, channels = frame.shape
    padded = jnp.pad(frame, ((1, 1), (1, 1), (0, 0)))
    running = jnp.zeros((rows * cols, channels), jnp.float32)
    for row_step in range(3):
        for col_step in range(3):
            window_piece = padded[row_step:row_step + rows, col_step:col_step + cols].reshape(rows * cols, channels)
            running = running + jnp.dot(window_piece, w_space[row_step, col_step], preferred_element_type=jnp.float32)
    return running.reshape(rows, cols, channels).astype(jnp.bfloat16)

def attend(block, w_qkv, w_out):
    frames, pixels, channels = block.shape
    head_size = channels // HEADS
    flattened = block.reshape(frames * pixels, channels)
    projected = jnp.dot(flattened, w_qkv, preferred_element_type=jnp.float32).astype(jnp.bfloat16)
    projected = projected.reshape(frames, pixels, 3, HEADS, head_size)
    query_rows = projected[:, :, 0].astype(jnp.float32)
    key_rows = projected[:, :, 1].astype(jnp.float32)
    value_rows = projected[:, :, 2].astype(jnp.float32)
    scores = jnp.einsum('fphd,gphd->phfg', query_rows, key_rows) / math.sqrt(head_size)
    weights = jax.nn.softmax(scores, axis=-1).astype(jnp.bfloat16)
    context = jnp.einsum('phfg,gphd->fphd', weights.astype(jnp.float32), value_rows).astype(jnp.bfloat16)
    context = context.reshape(frames * pixels, channels)
    result = flattened.astype(jnp.float32) + jnp.dot(context, w_out, preferred_element_type=jnp.float32)
    return result.reshape(frames, pixels, channels).astype(jnp.bfloat16)

def reference(video, w_space, w_time, norm_gain, norm_bias, w_qkv, w_out):
    spatial = lax.map(lambda frame: space_frame(frame, w_space), video)
    padded = jnp.pad(spatial, ((1, 1), (0, 0), (0, 0), (0, 0)))

    def time_frame(frame_index):
        window_piece = lax.dynamic_slice_in_dim(padded, frame_index, 3, 0)
        running = window_piece[1].astype(jnp.float32).reshape(HEIGHT * WIDTH, C)
        for tap in range(3):
            running = running + jnp.dot(window_piece[tap].reshape(HEIGHT * WIDTH, C), w_time[tap], preferred_element_type=jnp.float32)
        return running.reshape(HEIGHT, WIDTH, C).astype(jnp.bfloat16)
    temporal = lax.map(time_frame, jnp.arange(FRAMES).astype(jnp.int32))
    grouped = temporal.astype(jnp.float32).reshape(FRAMES * HEIGHT * WIDTH, GROUPS, C // GROUPS)
    cell_count = float(FRAMES * HEIGHT * WIDTH * (C // GROUPS))
    group_mean = lax.optimization_barrier(jnp.sum(grouped, axis=(0, 2))) / cell_count
    centered = grouped - group_mean[None, :, None]
    group_var = lax.optimization_barrier(jnp.sum(centered * centered, axis=(0, 2))) / cell_count
    scaled = centered * lax.rsqrt(group_var + 1e-05)[None, :, None]
    scaled = scaled.reshape(FRAMES * HEIGHT * WIDTH, C) * norm_gain + norm_bias
    normed = jax.nn.silu(scaled).astype(jnp.bfloat16).reshape(FRAMES, HEIGHT * WIDTH, C)
    block_rows = math.gcd(HEIGHT * WIDTH, 512)
    blocks = HEIGHT * WIDTH // block_rows
    stacked = normed.reshape(FRAMES, blocks, block_rows, C).transpose(1, 0, 2, 3)
    outcome = lax.map(lambda block: attend(block, w_qkv, w_out), stacked)
    return outcome.transpose(1, 0, 2, 3).reshape(FRAMES, HEIGHT, WIDTH, C)
```

```python
import functools
import math

import jax
import jax.numpy as jnp
from jax import lax
from jax.experimental import pallas as pl
from jax.experimental.pallas import tpu as pltpu
from jax.sharding import Mesh
from jax.sharding import PartitionSpec as P

HEADS = 8
GROUPS = 32
WIDTH = ("width_0", "width_1")
BF16 = jnp.bfloat16
F32 = jnp.float32
VMEM_BYTES = 60 * 1024 * 1024


def params(**kw):
    return pltpu.CompilerParams(vmem_limit_bytes=VMEM_BYTES, **kw)


def cost(flops, nbytes, trans=0):
    return pl.CostEstimate(flops=flops, bytes_accessed=nbytes, transcendentals=trans)


def shift(value, axis, step):
    size = lax.axis_size(axis)
    if step > 0:
        pairs = [(i, i + 1) for i in range(size - 1)]
    else:
        pairs = [(i + 1, i) for i in range(size - 1)]
    return lax.ppermute(value, axis, pairs)


def to_pixels(video):
    frames, rows, cols, channels = video.shape
    step = 4

    def kernel(v_ref, out_ref, first_ref, last_ref):
        for r in range(step):
            turned = jnp.swapaxes(v_ref[:, r], 0, 1)
            out_ref[r] = turned
            first_ref[r] = turned[0]
            last_ref[r] = turned[cols - 1]

    edge = jax.ShapeDtypeStruct((rows, frames, channels), BF16)
    return pl.pallas_call(
        kernel,
        grid=(rows // step,),
        in_specs=[pl.BlockSpec((frames, step, cols, channels), lambda i: (0, i, 0, 0))],
        out_specs=[
            pl.BlockSpec((step, cols, frames, channels), lambda i: (i, 0, 0, 0)),
            pl.BlockSpec((step, frames, channels), lambda i: (i, 0, 0)),
            pl.BlockSpec((step, frames, channels), lambda i: (i, 0, 0)),
        ],
        out_shape=[jax.ShapeDtypeStruct((rows, cols, frames, channels), BF16), edge, edge],
        compiler_params=params(),
        cost_estimate=cost(0, 2 * video.size * 2),
        name="to_pixels",
    )(video)


def spatial_conv(pixels, left, right, above, below, w_space):
    rows, cols, frames, channels = pixels.shape
    taps = 9
    span = 2
    count = span * cols * frames

    def kernel(p_ref, l_ref, r_ref, a_ref, b_ref, w_ref, out_ref, first_ref, last_ref, pad, acc):
        pad[0] = a_ref[...]
        pad[rows + 1] = b_ref[...]
        for r in range(rows):
            pad[r + 1, 0] = l_ref[r]
            pad[r + 1, pl.ds(1, cols)] = p_ref[r]
            pad[r + 1, cols + 1] = r_ref[r]

        def body(i, carry):
            base = i * span
            pieces = []
            for row_step in range(3):
                for col_step in range(3):
                    piece = pad[pl.ds(base + row_step, span), pl.ds(col_step, cols)]
                    pieces.append(piece.reshape(count, channels))
            window = jnp.concatenate(pieces, axis=1)
            total = jnp.dot(window, w_ref[...], preferred_element_type=F32)
            out_ref[pl.ds(base, span)] = total.astype(BF16).reshape(span, cols, frames, channels)
            for j in range(channels // 128):
                acc[j] = total[:, 128 * j : 128 * (j + 1)]
            chunk = span * cols
            for ref, frame in ((first_ref, 0), (last_ref, frames - 1)):
                picked = [
                    acc[j, pl.ds(frame, chunk, stride=frames)]
                    for j in range(channels // 128)
                ]
                ref[pl.ds(i * chunk, chunk)] = jnp.concatenate(picked, axis=1).astype(BF16)
            return carry

        lax.fori_loop(0, rows // span, body, 0)

    edge = jax.ShapeDtypeStruct((rows * cols, channels), BF16)
    size = rows * cols * frames * channels
    return pl.pallas_call(
        kernel,
        out_shape=[jax.ShapeDtypeStruct((rows, cols, frames, channels), BF16), edge, edge],
        scratch_shapes=[
            pltpu.VMEM((rows + 2, cols + 2, frames, channels), BF16),
            pltpu.VMEM((channels // 128, count, 128), F32),
        ],
        compiler_params=params(),
        cost_estimate=cost(2 * size * channels * taps, 4 * size),
        name="spatial_conv",
    )(pixels, left, right, above, below, w_space.reshape(taps * channels, channels))


def temporal_conv(me, spatial, before, after, w_time):
    pixels, frames, channels = spatial.shape
    parts = lax.axis_size("tm")
    quarter = pixels // parts
    chunk = 16
    count = chunk * frames
    per_group = channels // GROUPS

    def kernel(me_ref, s_ref, b_ref, a_ref, w_ref, *rest):
        outs, stats_ref = rest[:parts], rest[parts]
        row = lax.broadcasted_iota(jnp.int32, (count, channels), 0) % frames
        stats_ref[...] = jnp.zeros_like(stats_ref)
        for d in range(parts):
            start = lax.rem(me_ref[0] + d, parts) * quarter

            def body(i, carry):
                base = start + i * chunk
                x = s_ref[pl.ds(base, chunk)].reshape(count, channels)
                xf = x.astype(F32)
                prev = b_ref[pl.ds(pl.multiple_of(base, chunk), chunk)].astype(F32)
                nxt = a_ref[pl.ds(pl.multiple_of(base, chunk), chunk)].astype(F32)
                shape = (chunk, frames, channels)
                prev = jnp.broadcast_to(prev[:, None, :], shape).reshape(count, channels)
                nxt = jnp.broadcast_to(nxt[:, None, :], shape).reshape(count, channels)
                down = jnp.where(row == 0, prev, pltpu.roll(xf, 1, 0)).astype(BF16)
                up = jnp.where(row == frames - 1, nxt, pltpu.roll(xf, count - 1, 0)).astype(BF16)
                window = jnp.concatenate([down, x, up], axis=1)
                total = xf + jnp.dot(window, w_ref[...], preferred_element_type=F32)
                rounded = total.astype(BF16)
                outs[d][pl.ds(i * chunk, chunk)] = rounded.reshape(shape)
                kept = rounded.astype(F32)
                stats_ref[0:1] += jnp.sum(kept, axis=0, keepdims=True)
                stats_ref[1:2] += jnp.sum(kept * kept, axis=0, keepdims=True)
                return carry

            lax.fori_loop(0, quarter // chunk, body, 0)
        same = (
            lax.broadcasted_iota(jnp.int32, (channels, channels), 0) // per_group
            == lax.broadcasted_iota(jnp.int32, (channels, channels), 1) // per_group
        ).astype(F32)
        stats_ref[...] = jnp.dot(
            stats_ref[...], same, precision=lax.Precision.HIGHEST, preferred_element_type=F32
        )

    vmem = pl.BlockSpec(memory_space=pltpu.VMEM)
    size = pixels * frames * channels
    res = pl.pallas_call(
        kernel,
        in_specs=[pl.BlockSpec(memory_space=pltpu.SMEM)] + [vmem] * 4,
        out_specs=[vmem] * (parts + 1),
        out_shape=[jax.ShapeDtypeStruct((quarter, frames, channels), BF16)] * parts
        + [jax.ShapeDtypeStruct((8, channels), F32)],
        compiler_params=params(),
        cost_estimate=cost(2 * size * channels * 3, 4 * size),
        name="temporal_conv",
    )(me, spatial, before, after, w_time.reshape(3 * channels, channels))
    return res[:parts], res[parts]


def attention(blocks, stats, gain, bias, w_qkv, w_out, cell_count):
    parts = len(blocks)
    pixels, frames, channels = blocks[0].shape
    length = parts * frames
    group = 8
    head = channels // HEADS
    half = channels // 2
    per_half = HEADS // 2
    factor = math.log2(math.e) / math.sqrt(head)

    def kernel(*refs):
        ins, refs = refs[:parts], refs[parts:]
        stats_ref, gain_ref, bias_ref, qkv_ref, out_w_ref = refs[:5]
        outs = refs[5:]
        mean = stats_ref[0:1] / cell_count
        var = jnp.maximum(stats_ref[1:2] / cell_count - mean * mean, 0.0)
        scale = lax.rsqrt(var + 1e-05) * gain_ref[...]
        x = jnp.concatenate([ref[...] for ref in ins], axis=1).astype(F32)
        x = x.reshape(group * length, channels)
        v = (x - mean) * scale + bias_ref[...]
        normed = (v * (0.5 + 0.5 * jnp.tanh(0.5 * v))).astype(BF16)
        projected = jnp.dot(normed, qkv_ref[...], preferred_element_type=F32).astype(BF16)
        lane = lax.broadcasted_iota(jnp.int32, (length, channels), 1)
        halves = [(lane // half) == i for i in range(2)]
        heads = [((lane // head) % per_half) == i for i in range(per_half)]
        zero = jnp.zeros((length, channels), BF16)
        contexts = []
        for g in range(group):
            rows = slice(g * length, (g + 1) * length)
            q = projected[rows, :channels]
            k = projected[rows, channels : 2 * channels]
            val = projected[rows, 2 * channels :]
            qm = jnp.concatenate([jnp.where(m, q, zero) for m in halves], axis=0)
            km = jnp.concatenate([jnp.where(m, k, zero) for m in heads], axis=0)
            vm = jnp.concatenate([jnp.where(m, val, zero) for m in heads], axis=0)
            scores = lax.dot_general(
                km, qm, (((1,), (1,)), ((), ())), preferred_element_type=F32
            ).reshape(per_half, length, 2 * length)
            top = jnp.max(scores, axis=1, keepdims=True)
            e = jnp.exp2((scores - top) * factor)
            weights = (e * (1.0 / jnp.sum(e, axis=1, keepdims=True))).astype(BF16)
            mixed = lax.dot_general(
                weights.reshape(per_half * length, 2 * length),
                vm,
                (((0,), (0,)), ((), ())),
                preferred_element_type=F32,
            )
            contexts.append(
                jnp.concatenate([mixed[:length, :half], mixed[length:, half:]], axis=1).astype(BF16)
            )
        context = jnp.concatenate(contexts, axis=0)
        result = normed.astype(F32) + jnp.dot(
            context, out_w_ref[...], preferred_element_type=F32
        )
        result = result.astype(BF16).reshape(group, parts, frames, channels)
        for d in range(parts):
            outs[d][...] = result[:, d]

    block = pl.BlockSpec((group, frames, channels), lambda i: (i, 0, 0))

    def whole(a):
        return pl.BlockSpec(a.shape, lambda i: (0,) * a.ndim)

    rest = (stats, gain, bias, w_qkv, w_out)
    size = parts * pixels * frames * channels
    return pl.pallas_call(
        kernel,
        grid=(pixels // group,),
        in_specs=[block] * parts + [whole(a) for a in rest],
        out_specs=[block] * parts,
        out_shape=[jax.ShapeDtypeStruct((pixels, frames, channels), BF16)] * parts,
        compiler_params=params(),
        cost_estimate=cost(2 * size * channels * 8, 4 * size, size * 3),
        name="attention",
    )(*blocks, *rest)


def from_pixels(me, blocks, rows, cols):
    parts = len(blocks)
    pixels, frames, channels = blocks[0].shape
    part_rows = pixels // cols

    def kernel(me_ref, *refs):
        ins, out_ref = refs[:parts], refs[parts]
        for d in range(parts):
            base = lax.rem(me_ref[0] + d, parts) * part_rows
            for r in range(part_rows):
                out_ref[:, base + r] = jnp.swapaxes(ins[d][pl.ds(r * cols, cols)], 0, 1)

    vmem = pl.BlockSpec(memory_space=pltpu.VMEM)
    return pl.pallas_call(
        kernel,
        in_specs=[pl.BlockSpec(memory_space=pltpu.SMEM)] + [vmem] * parts,
        out_specs=vmem,
        out_shape=jax.ShapeDtypeStruct((frames, rows, cols, channels), BF16),
        compiler_params=params(),
        cost_estimate=cost(0, 4 * parts * pixels * frames * channels),
        name="from_pixels",
    )(me, *blocks)


def rotate(value, step):
    size = lax.axis_size("tm")
    return lax.ppermute(value, "tm", [(i, (i + step) % size) for i in range(size)])


def summed(stats):
    for axis in ("width_1", "tm", "height", "width_0"):
        size = lax.axis_size(axis)
        step = 1
        while step < size:
            stats = stats + lax.ppermute(stats, axis, [(i, i ^ step) for i in range(size)])
            step *= 2
    return stats


def per_device(video, w_space, w_time, norm_gain, norm_bias, w_qkv, w_out):
    frames, rows, cols, channels = video.shape
    parts = lax.axis_size("tm")
    me = lax.axis_index("tm").astype(jnp.int32).reshape(1)
    pixels, first, last = to_pixels(video)
    left = shift(last, WIDTH, 1)
    right = shift(first, WIDTH, -1)

    def border(r):
        return jnp.concatenate([left[r][None], pixels[r], right[r][None]], axis=0)

    above = shift(border(rows - 1), "height", 1)
    below = shift(border(0), "height", -1)
    spatial, early, late = spatial_conv(pixels, left, right, above, below, w_space)
    before = shift(late, "tm", 1)
    after = shift(early, "tm", -1)
    blocks, stats = temporal_conv(
        me, spatial.reshape(rows * cols, frames, channels), before, after, w_time
    )
    moved = [blocks[0]] + [rotate(blocks[d], d) for d in range(1, parts)]
    stats = summed(stats)
    cell_count = float(
        frames * parts * rows * lax.axis_size("height") * cols * lax.axis_size(WIDTH)
        * (channels // GROUPS)
    )
    results = attention(
        moved, stats, norm_gain.reshape(1, -1), norm_bias.reshape(1, -1), w_qkv, w_out, cell_count
    )
    back = [results[0]] + [rotate(results[d], -d) for d in range(1, parts)]
    return from_pixels(me, back, rows, cols)


def solution(mesh):
    torus = Mesh(
        mesh.devices.reshape(mesh.shape["tm"], mesh.shape["height"], 8, 2),
        ("tm", "height", "width_0", "width_1"),
    )
    in_specs = (P("tm", "height", WIDTH, None), P(), P(), P(), P(), P(), P())
    out_specs = P("tm", "height", WIDTH, None)
    return jax.shard_map(
        per_device, mesh=torus, in_specs=in_specs, out_specs=out_specs, check_vma=False
    )
```

```python
import math

import jax
import jax.numpy as jnp
from jax import lax
from jax.experimental import pallas as pl
from jax.experimental.pallas import tpu as pltpu
from jax.sharding import Mesh
from jax.sharding import PartitionSpec as P

HEADS = 8
GROUPS = 32
WIDTH = ("width_0", "width_1")
BF16 = jnp.bfloat16
F32 = jnp.float32
VMEM_BYTES = 60 * 1024 * 1024


def params(**kw):
    return pltpu.CompilerParams(vmem_limit_bytes=VMEM_BYTES, **kw)


def cost(flops, nbytes, trans=0):
    return pl.CostEstimate(flops=flops, bytes_accessed=nbytes, transcendentals=trans)


def shift(value, axis, step):
    size = lax.axis_size(axis)
    if step > 0:
        pairs = [(i, i + 1) for i in range(size - 1)]
    else:
        pairs = [(i + 1, i) for i in range(size - 1)]
    return lax.ppermute(value, axis, pairs)


def edge_columns(video):
    frames, rows, cols, channels = video.shape
    step = 4

    def kernel(v_ref, first_ref, last_ref):
        for r in range(step):
            turned = jnp.swapaxes(v_ref[:, r], 0, 1)
            first_ref[r] = turned[0]
            last_ref[r] = turned[cols - 1]

    return pl.pallas_call(
        kernel,
        grid=(rows // step,),
        in_specs=[pl.BlockSpec((frames, step, cols, channels), lambda i: (0, i, 0, 0))],
        out_specs=[pl.BlockSpec((step, frames, channels), lambda i: (i, 0, 0))] * 2,
        out_shape=[jax.ShapeDtypeStruct((rows, frames, channels), BF16)] * 2,
        compiler_params=params(),
        cost_estimate=cost(0, video.size * 2),
        name="edge_columns",
    )(video)


def to_pixels(video):
    frames, rows, cols, channels = video.shape
    step = 4

    def kernel(v_ref, out_ref):
        for r in range(step):
            out_ref[r] = jnp.swapaxes(v_ref[:, r], 0, 1)

    return pl.pallas_call(
        kernel,
        grid=(rows // step,),
        in_specs=[pl.BlockSpec((frames, step, cols, channels), lambda i: (0, i, 0, 0))],
        out_specs=pl.BlockSpec((step, cols, frames, channels), lambda i: (i, 0, 0, 0)),
        out_shape=jax.ShapeDtypeStruct((rows, cols, frames, channels), BF16),
        compiler_params=params(),
        cost_estimate=cost(0, 2 * video.size * 2),
        name="to_pixels",
    )(video)


def convolve(pad, base, span, cols, w_ref):
    pieces = []
    for row_step in range(3):
        for col_step in range(3):
            piece = pad[pl.ds(base + row_step, span), pl.ds(col_step, cols)]
            pieces.append(piece.reshape(span * cols * piece.shape[2], piece.shape[3]))
    window = jnp.concatenate(pieces, axis=1)
    return jnp.dot(window, w_ref[...], preferred_element_type=F32)


def end_frames(acc, total, frames, count):
    slabs = total.shape[1] // 128
    for j in range(slabs):
        acc[j] = total[:, 128 * j : 128 * (j + 1)]
    return [
        jnp.concatenate(
            [acc[j, pl.ds(frame, count, stride=frames)] for j in range(slabs)], axis=1
        ).astype(BF16)
        for frame in (0, frames - 1)
    ]


def inner_conv(pixels, left, right, w_space):
    rows, cols, frames, channels = pixels.shape
    span = 2
    chunk = span * cols
    count = chunk * frames

    def kernel(p_ref, l_ref, r_ref, w_ref, out_ref, first_ref, last_ref, pad, acc):
        for r in range(rows):
            pad[r, 0] = l_ref[r]
            pad[r, pl.ds(1, cols)] = p_ref[r]
            pad[r, cols + 1] = r_ref[r]

        def body(i, carry):
            base = i * span
            total = convolve(pad, base, span, cols, w_ref)
            out_ref[pl.ds(base + 1, span)] = total.astype(BF16).reshape(span, cols, frames, channels)
            ends = end_frames(acc, total, frames, chunk)
            for ref, value in zip((first_ref, last_ref), ends):
                ref[pl.ds(pl.multiple_of(base * cols + cols, cols), chunk)] = value
            return carry

        lax.fori_loop(0, (rows - 2) // span, body, 0)

    edge = jax.ShapeDtypeStruct((rows * cols, channels), BF16)
    size = (rows - 2) * cols * frames * channels
    return pl.pallas_call(
        kernel,
        out_shape=[jax.ShapeDtypeStruct((rows, cols, frames, channels), BF16), edge, edge],
        scratch_shapes=[
            pltpu.VMEM((rows, cols + 2, frames, channels), BF16),
            pltpu.VMEM((channels // 128, count, 128), F32),
        ],
        compiler_params=params(),
        cost_estimate=cost(2 * size * channels * 9, 4 * size),
        name="inner_conv",
    )(pixels, left, right, w_space)


def outer_conv(pixels, left, right, above, below, w_space, results):
    rows, cols, frames, channels = pixels.shape
    count = cols * frames

    def kernel(p_ref, l_ref, r_ref, a_ref, b_ref, w_ref, *refs):
        outs, (pad, acc, wide, ends, sem) = refs[3:6], refs[6:]
        fetch = [
            pltpu.make_async_copy(
                p_ref.at[pl.ds(start, 2)], pad.at[pl.ds(to, 2), pl.ds(1, cols)], sem.at[i]
            )
            for i, (start, to) in enumerate(((0, 1), (rows - 2, 3)))
        ]
        for copy in fetch:
            copy.start()
        pad[0] = a_ref[...]
        pad[5] = b_ref[...]
        for r, to in ((0, 1), (1, 2), (rows - 2, 3), (rows - 1, 4)):
            pad[to, 0] = l_ref[r]
            pad[to, cols + 1] = r_ref[r]
        for copy in fetch:
            copy.wait()
        copies = []
        for k, row in enumerate((0, rows - 1)):
            total = convolve(pad, 3 * k, 1, cols, w_ref)
            wide[k] = total.astype(BF16).reshape(cols, frames, channels)
            for e, value in enumerate(end_frames(acc.at[k], total, frames, cols)):
                ends[k, e] = value
            copies.append((wide.at[k], outs[0].at[row]))
            for e in range(2):
                copies.append((ends.at[k, e], outs[1 + e].at[pl.ds(row * cols, cols)]))
        started = []
        for i, (source, target) in enumerate(copies):
            copy = pltpu.make_async_copy(source, target, sem.at[2 + i])
            copy.start()
            started.append(copy)
        for copy in started:
            copy.wait()

    anywhere = pl.BlockSpec(memory_space=pl.ANY)
    vmem = pl.BlockSpec(memory_space=pltpu.VMEM)
    size = 2 * cols * frames * channels
    return pl.pallas_call(
        kernel,
        in_specs=[anywhere] + [vmem] * 5 + [anywhere] * 3,
        out_specs=[anywhere] * 3,
        out_shape=[jax.ShapeDtypeStruct(a.shape, a.dtype) for a in results],
        input_output_aliases={6: 0, 7: 1, 8: 2},
        scratch_shapes=[
            pltpu.VMEM((6, cols + 2, frames, channels), BF16),
            pltpu.VMEM((2, channels // 128, count, 128), F32),
            pltpu.VMEM((2, cols, frames, channels), BF16),
            pltpu.VMEM((2, 2, cols, channels), BF16),
            pltpu.SemaphoreType.DMA((8,)),
        ],
        compiler_params=params(),
        cost_estimate=cost(2 * size * channels * 9, 4 * size),
        name="outer_conv",
    )(pixels, left, right, above, below, w_space, *results)


def group_lanes(channels):
    shape = (channels, 128)
    channel = lax.broadcasted_iota(jnp.int32, shape, 0)
    lane = lax.broadcasted_iota(jnp.int32, shape, 1)
    return (channel // (channels // GROUPS) == lane).astype(F32)


def temporal_conv(me, spatial, before, after, w_time):
    pixels, frames, channels = spatial.shape
    parts = lax.axis_size("tm")
    quarter = pixels // parts
    chunk = 16
    count = chunk * frames
    lanes = 128
    slabs = channels // lanes
    pitch = frames + 8
    per_part = quarter // chunk
    steps = parts * per_part

    def kernel(me_ref, s_ref, b_ref, a_ref, w_ref, *rest):
        outs, stats_ref = rest[:parts], rest[parts]
        wides, windows, totals = rest[parts + 1 : parts + 3], rest[parts + 3 : parts + 5], rest[parts + 5 :]

        def base_of(t):
            start = lax.rem(me_ref[0] + t // per_part, parts) * quarter
            return pl.multiple_of(start + (t % per_part) * chunk, chunk)

        def prepare(t):
            base = base_of(t)
            wide, window = wides[t % 2], windows[t % 2]
            x = s_ref[pl.ds(base, chunk)].reshape(count, channels)
            xf = x.astype(F32)
            prev = b_ref[pl.ds(base, chunk)].astype(F32)
            nxt = a_ref[pl.ds(base, chunk)].astype(F32)
            window[:, channels : 2 * channels] = x
            for j in range(slabs):
                cut = slice(j * lanes, (j + 1) * lanes)
                wide[j, pl.ds(7, chunk, stride=pitch)] = prev[:, cut]
                wide[j, pl.ds(pitch, chunk, stride=pitch)] = nxt[:, cut]
                for p in range(chunk):
                    wide[j, pl.ds(p * pitch + 8, frames)] = xf[p * frames : (p + 1) * frames, cut]
            for p in range(chunk):
                for j in range(slabs):
                    for offset, to in ((7, 0), (9, 2)):
                        window[
                            p * frames : (p + 1) * frames,
                            to * channels + j * lanes : to * channels + (j + 1) * lanes,
                        ] = wide[j, pl.ds(p * pitch + offset, frames)].astype(BF16)

        def multiply(t):
            window = windows[t % 2]
            totals[t % 2][...] = jnp.dot(window[...], w_ref[...], preferred_element_type=F32)

        def finish(t, sums):
            x = s_ref[pl.ds(base_of(t), chunk)].reshape(count, channels).astype(F32)
            rounded = (x + totals[t % 2][...]).astype(BF16)
            outs[t // per_part][pl.ds(t % per_part * chunk, chunk)] = rounded.reshape(
                chunk, frames, channels
            )
            kept = rounded.astype(F32).reshape(count // 8, 8, channels)
            return sums[0] + jnp.sum(kept, axis=0), sums[1] + jnp.sum(kept * kept, axis=0)

        sums = (jnp.zeros((8, channels), F32),) * 2
        prepare(0)
        for t in range(steps + 1):
            if t < steps:
                multiply(t)
            if t + 1 < steps:
                prepare(t + 1)
            if t > 0:
                sums = finish(t - 1, sums)
        folded = [jnp.sum(v, axis=0, keepdims=True) for v in sums] + [jnp.zeros((6, channels), F32)]
        stats_ref[...] = jnp.dot(
            jnp.concatenate(folded, axis=0),
            group_lanes(channels),
            precision=lax.Precision.HIGHEST,
            preferred_element_type=F32,
        )

    vmem = pl.BlockSpec(memory_space=pltpu.VMEM)
    size = pixels * frames * channels
    res = pl.pallas_call(
        kernel,
        in_specs=[pl.BlockSpec(memory_space=pltpu.SMEM)] + [vmem] * 4,
        out_specs=[vmem] * (parts + 1),
        out_shape=[jax.ShapeDtypeStruct((quarter, frames, channels), BF16)] * parts
        + [jax.ShapeDtypeStruct((8, 128), F32)],
        scratch_shapes=[pltpu.VMEM((slabs, chunk * pitch + 8, lanes), F32)] * 2
        + [pltpu.VMEM((count, 3 * channels), BF16)] * 2
        + [pltpu.VMEM((count, channels), F32)] * 2,
        compiler_params=params(),
        cost_estimate=cost(2 * size * channels * 3, 4 * size),
        name="temporal_conv",
    )(me, spatial, before, after, w_time.reshape(3 * channels, channels))
    return res[:parts], res[parts]


def attention(blocks, stats, gain, bias, w_qkv, w_out, cell_count, first, pixels):
    parts = len(blocks)
    frames, channels = blocks[0].shape[1:]
    length = parts * frames
    group = 8
    head = channels // HEADS
    half = channels // 2
    per_half = HEADS // 2
    factor = math.log2(math.e) / math.sqrt(head)
    batch = 4

    def kernel(*refs):
        ins, refs = refs[:parts], refs[parts:]
        stats_ref, gain_ref, bias_ref, qkv_ref, out_w_ref = refs[:5]
        outs, refs = refs[5 : 5 + parts], refs[5 + parts :]
        normed, projected, contexts, affine = refs[:2], refs[2:4], refs[4], refs[5]
        spread = lax.dot_general(
            stats_ref[...],
            group_lanes(channels),
            (((1,), (1,)), ((), ())),
            precision=lax.Precision.HIGHEST,
            preferred_element_type=F32,
        )
        mean = spread[0:1] / cell_count
        var = jnp.maximum(spread[1:2] / cell_count - mean * mean, 0.0)
        scale = 0.5 * lax.rsqrt(var + 1e-05) * gain_ref[...]
        affine[0:8] = jnp.broadcast_to(scale, (8, channels))
        affine[8:16] = jnp.broadcast_to(0.5 * bias_ref[...] - mean * scale, (8, channels))
        lane = lax.broadcasted_iota(jnp.int32, (length, channels), 1)
        halves = [(lane // half) == i for i in range(2)]
        heads = [((lane // head) % per_half) == i for i in range(per_half)]

        def normalize(slot, pixel, g):
            x = jnp.concatenate([ref[pixel + g] for ref in ins], axis=0).astype(F32)
            x = x.reshape(length // 8, 8, channels)
            u = (x * affine[0:8][None] + affine[8:16][None]).reshape(length, channels)
            normed[slot][g * length : (g + 1) * length] = (u + u * jnp.tanh(u)).astype(BF16)

        def project(slot, b):
            rows = slice(b * batch * length, (b + 1) * batch * length)
            projected[slot][rows] = jnp.dot(
                normed[slot][rows], qkv_ref[...], preferred_element_type=F32
            ).astype(BF16)

        zero = jnp.zeros((length, channels), BF16)

        def score(slot, g):
            rows = slice(g * length, (g + 1) * length)
            q = projected[slot][rows, :channels]
            k = projected[slot][rows, channels : 2 * channels]
            qm = jnp.concatenate([jnp.where(m, q, zero) for m in halves], axis=0)
            km = jnp.concatenate([jnp.where(m, k, zero) for m in heads], axis=0)
            return lax.dot_general(
                km, qm, (((1,), (1,)), ((), ())), preferred_element_type=F32
            ).reshape(per_half, length, 2 * length)

        def soften(scores):
            top = jnp.max(scores, axis=1, keepdims=True)
            e = jnp.exp2((scores - top) * factor)
            weights = (e * (1.0 / jnp.sum(e, axis=1, keepdims=True))).astype(BF16)
            return weights.reshape(per_half * length, 2 * length)

        def mix(slot, g, weights):
            rows = slice(g * length, (g + 1) * length)
            val = projected[slot][rows, 2 * channels :]
            vm = jnp.concatenate([jnp.where(m, val, zero) for m in heads], axis=0)
            mixed = lax.dot_general(
                weights, vm, (((0,), (0,)), ((), ())), preferred_element_type=F32
            )
            contexts[rows] = jnp.concatenate(
                [mixed[:length, :half], mixed[length:, half:]], axis=1
            ).astype(BF16)

        def finish(slot, pixel, b):
            rows = slice(b * batch * length, (b + 1) * batch * length)
            result = normed[slot][rows].astype(F32) + jnp.dot(
                contexts[rows], out_w_ref[...], preferred_element_type=F32
            )
            result = result.astype(BF16).reshape(batch, parts, frames, channels)
            for d in range(parts):
                outs[d][pl.ds(pixel - first + b * batch, batch)] = result[:, d]

        def work(slot, pixel, ahead):
            scores, weights = {}, {}
            for t in range(group + 2):
                if t < group:
                    scores[t] = score(slot, t)
                    normalize(1 - slot, ahead, t)
                    if (t + 1) % batch == 0:
                        project(1 - slot, t // batch)
                if 0 <= t - 1 < group:
                    weights[t - 1] = soften(scores.pop(t - 1))
                if 0 <= t - 2 < group:
                    mix(slot, t - 2, weights.pop(t - 2))
                    if (t - 1) % batch == 0:
                        finish(slot, pixel, (t - 2) // batch)

        for g in range(group):
            normalize(0, first, g)
        for b in range(group // batch):
            project(0, b)

        def body(i, carry):
            pixel = first + i * 2 * group
            work(0, pixel, pixel + group)
            ahead = jnp.minimum(pixel + 2 * group, first + pixels - group)
            work(1, pixel + group, ahead)
            return carry

        lax.fori_loop(0, pixels // (2 * group), body, 0)

    rest = (stats, gain, bias, w_qkv, w_out)
    vmem = pl.BlockSpec(memory_space=pltpu.VMEM)
    size = parts * pixels * frames * channels
    return pl.pallas_call(
        kernel,
        in_specs=[vmem] * (parts + len(rest)),
        out_specs=[vmem] * parts,
        out_shape=[jax.ShapeDtypeStruct((pixels, frames, channels), BF16)] * parts,
        scratch_shapes=[pltpu.VMEM((group * length, channels), BF16)] * 2
        + [pltpu.VMEM((group * length, 3 * channels), BF16)] * 2
        + [pltpu.VMEM((group * length, channels), BF16), pltpu.VMEM((16, channels), F32)],
        compiler_params=params(),
        cost_estimate=cost(2 * size * channels * 8, 4 * size, size * 3),
        name="attention",
    )(*blocks, *rest)


def from_pixels(me, halves, rows, cols):
    parts = len(halves[0])
    pixels, frames, channels = halves[0][0].shape
    half_rows = pixels // cols
    part_rows = half_rows * len(halves)
    flat = [block for blocks in halves for block in blocks]
    total = len(flat) * half_rows

    def kernel(me_ref, *refs):
        ins, out_ref, turned, sem = refs[: len(flat)], refs[-3], refs[-2], refs[-1]
        copies = []
        for h in range(len(halves)):
            for d in range(parts):
                base = lax.rem(me_ref[0] + d, parts) * part_rows + h * half_rows
                for r in range(half_rows):
                    slot = len(copies)
                    turned[slot] = jnp.swapaxes(ins[h * parts + d][pl.ds(r * cols, cols)], 0, 1)
                    copy = pltpu.make_async_copy(
                        turned.at[slot], out_ref.at[:, base + r], sem.at[slot]
                    )
                    copy.start()
                    copies.append(copy)
        for copy in copies:
            copy.wait()

    vmem = pl.BlockSpec(memory_space=pltpu.VMEM)
    return pl.pallas_call(
        kernel,
        in_specs=[pl.BlockSpec(memory_space=pltpu.SMEM)] + [vmem] * len(flat),
        out_specs=pl.BlockSpec(memory_space=pl.ANY),
        out_shape=jax.ShapeDtypeStruct((frames, rows, cols, channels), BF16),
        scratch_shapes=[
            pltpu.VMEM((total, frames, cols, channels), BF16),
            pltpu.SemaphoreType.DMA((total,)),
        ],
        compiler_params=params(),
        cost_estimate=cost(0, 4 * frames * rows * cols * channels),
        name="from_pixels",
    )(me, *flat)


def rotate(value, step):
    size = lax.axis_size("tm")
    return lax.ppermute(value, "tm", [(i, (i + step) % size) for i in range(size)])


def per_device(video, w_space, w_time, norm_gain, norm_bias, w_qkv, w_out):
    frames, rows, cols, channels = video.shape
    parts = lax.axis_size("tm")
    me = lax.axis_index("tm").astype(jnp.int32).reshape(1)
    first, last = edge_columns(video)
    left = shift(last, WIDTH, 1)
    right = shift(first, WIDTH, -1)
    pixels = to_pixels(video)

    def border(r):
        return jnp.concatenate([left[r][None], pixels[r], right[r][None]], axis=0)

    above = shift(border(rows - 1), "height", 1)
    below = shift(border(0), "height", -1)
    taps = w_space.reshape(9 * channels, channels)
    inner = inner_conv(pixels, left, right, taps)
    spatial, early, late = outer_conv(pixels, left, right, above, below, taps, inner)
    before = shift(late, "tm", 1)
    after = shift(early, "tm", -1)
    blocks, stats = temporal_conv(
        me, spatial.reshape(rows * cols, frames, channels), before, after, w_time
    )
    stats = stats + sum(rotate(stats, d) for d in range(1, parts))
    moved = [blocks[0]]
    for d in range(1, parts):
        moved.append(rotate(blocks[d], d))
    stats = stats + lax.ppermute(stats, "width_1", [(0, 1), (1, 0)])
    others = ("height", "width_0")
    count = lax.axis_size(others)
    shared = jnp.broadcast_to(stats[None], (count, *stats.shape))
    stats = jnp.sum(lax.all_to_all(shared, others, 0, 0), axis=0)
    cell_count = float(
        frames * parts * rows * lax.axis_size("height") * cols * lax.axis_size(WIDTH)
        * (channels // GROUPS)
    )
    weights = (norm_gain.reshape(1, -1), norm_bias.reshape(1, -1), w_qkv, w_out)
    share = rows * cols // parts // 2
    halves = []
    for h in range(2):
        results = attention(moved, stats, *weights, cell_count, h * share, share)
        halves.append([results[0]] + [rotate(results[d], -d) for d in range(1, parts)])
    return from_pixels(me, halves, rows, cols)


def solution(mesh):
    torus = Mesh(
        mesh.devices.reshape(mesh.shape["tm"], mesh.shape["height"], 8, 2),
        ("tm", "height", "width_0", "width_1"),
    )
    in_specs = (P("tm", "height", WIDTH, None), P(), P(), P(), P(), P(), P())
    out_specs = P("tm", "height", WIDTH, None)
    return jax.shard_map(
        per_device, mesh=torus, in_specs=in_specs, out_specs=out_specs, check_vma=False
    )
```

```python
import math

import jax
import jax.numpy as jnp
from jax import lax
from jax.experimental import pallas as pl
from jax.experimental.pallas import tpu as pltpu
from jax.sharding import Mesh
from jax.sharding import PartitionSpec as P

HEADS = 8
GROUPS = 32
WIDTH = ("width_0", "width_1")
BF16 = jnp.bfloat16
F32 = jnp.float32
VMEM_BYTES = 60 * 1024 * 1024


def params(**kw):
    return pltpu.CompilerParams(vmem_limit_bytes=VMEM_BYTES, **kw)


def cost(flops, nbytes, trans=0):
    return pl.CostEstimate(flops=flops, bytes_accessed=nbytes, transcendentals=trans)


def shift(value, axis, step):
    size = lax.axis_size(axis)
    if step > 0:
        pairs = [(i, i + 1) for i in range(size - 1)]
    else:
        pairs = [(i + 1, i) for i in range(size - 1)]
    return lax.ppermute(value, axis, pairs)


def to_pixels(video):
    frames, rows, cols, channels = video.shape
    step = 4

    def kernel(v_ref, out_ref):
        for r in range(step):
            out_ref[r] = jnp.swapaxes(v_ref[:, r], 0, 1)

    return pl.pallas_call(
        kernel,
        grid=(rows // step,),
        in_specs=[pl.BlockSpec((frames, step, cols, channels), lambda i: (0, i, 0, 0))],
        out_specs=pl.BlockSpec((step, cols, frames, channels), lambda i: (i, 0, 0, 0)),
        out_shape=jax.ShapeDtypeStruct((rows, cols, frames, channels), BF16),
        compiler_params=params(),
        cost_estimate=cost(0, 2 * video.size * 2),
        name="to_pixels",
    )(video)


def spatial_conv(pixels, left, right, above, below, w_space):
    rows, cols, frames, channels = pixels.shape
    span = 2
    count = span * cols * frames
    unroll = 2

    def kernel(p_ref, l_ref, r_ref, a_ref, b_ref, w_ref, out_ref, pad):
        pad[0] = a_ref[...]
        pad[rows + 1] = b_ref[...]
        for r in range(rows):
            pad[r + 1, 0] = l_ref[r]
            pad[r + 1, pl.ds(1, cols)] = p_ref[r]
            pad[r + 1, cols + 1] = r_ref[r]

        def body(i, carry):
            for u in range(unroll):
                base = (i * unroll + u) * span
                pieces = []
                for row_step in range(3):
                    for col_step in range(3):
                        piece = pad[pl.ds(base + row_step, span), pl.ds(col_step, cols)]
                        pieces.append(piece.reshape(count, channels))
                window = jnp.concatenate(pieces, axis=1)
                total = jnp.dot(window, w_ref[...], preferred_element_type=F32)
                out_ref[pl.ds(base, span)] = total.astype(BF16).reshape(
                    span, cols, frames, channels
                )
            return carry

        lax.fori_loop(0, rows // span // unroll, body, 0)

    size = rows * cols * frames * channels
    return pl.pallas_call(
        kernel,
        out_shape=jax.ShapeDtypeStruct((rows, cols, frames, channels), BF16),
        scratch_shapes=[pltpu.VMEM((rows + 2, cols + 2, frames, channels), BF16)],
        compiler_params=params(),
        cost_estimate=cost(2 * size * channels * 9, 4 * size),
        name="spatial_conv",
    )(pixels, left, right, above, below, w_space)


def end_frames(video, left, right, above, below, w_space):
    frames, rows, cols, channels = video.shape
    lanes = 128
    slabs = channels // lanes
    pitch = cols + 8
    taps = 9
    ends = (0, frames - 1)

    def kernel(v_ref, l_ref, r_ref, a_ref, b_ref, w_ref, early_ref, late_ref, held, side, wide, window, sem):
        fetch = [
            pltpu.make_async_copy(v_ref.at[frame], held.at[k], sem.at[k])
            for k, frame in enumerate(ends)
        ]
        for copy in fetch:
            copy.start()
        for j in range(slabs):
            cut = slice(j * lanes, (j + 1) * lanes)
            for n, ref in enumerate((l_ref, r_ref, a_ref, b_ref)):
                size = ref.shape[0] * frames
                side[n, j, pl.ds(0, size)] = ref[...].reshape(size, channels)[:, cut].astype(F32)
        for copy in fetch:
            copy.wait()
        outs = (early_ref, late_ref)
        for k, frame in enumerate(ends):
            for j in range(slabs):
                cut = slice(j * lanes, (j + 1) * lanes)
                for n, at in ((0, 7), (1, pitch)):
                    wide[k, j, pl.ds(pitch + at, rows, stride=pitch)] = side[
                        n, j, pl.ds(frame, rows, stride=frames)
                    ]
                for n, row in ((2, 0), (3, rows + 1)):
                    wide[k, j, pl.ds(row * pitch + 7, cols + 2)] = side[
                        n, j, pl.ds(frame, cols + 2, stride=frames)
                    ]
                for r in range(rows):
                    wide[k, j, pl.ds((r + 1) * pitch + 8, cols)] = held[k, r, :, cut].astype(F32)
            for tap in range(taps):
                row_step, col_step = tap // 3, tap % 3
                for r in range(rows):
                    for j in range(slabs):
                        at = tap * channels + j * lanes
                        window[k, r * cols : (r + 1) * cols, at : at + lanes] = wide[
                            k, j, pl.ds((r + row_step) * pitch + 7 + col_step, cols)
                        ].astype(BF16)
            outs[k][...] = jnp.dot(
                window[k], w_ref[...], preferred_element_type=F32
            ).astype(BF16)

    anywhere = pl.BlockSpec(memory_space=pl.ANY)
    vmem = pl.BlockSpec(memory_space=pltpu.VMEM)
    size = 2 * rows * cols * channels
    return pl.pallas_call(
        kernel,
        in_specs=[anywhere] + [vmem] * 5,
        out_specs=[vmem] * 2,
        out_shape=[jax.ShapeDtypeStruct((rows * cols, channels), BF16)] * 2,
        scratch_shapes=[
            pltpu.VMEM((2, rows, cols, channels), BF16),
            pltpu.VMEM((4, slabs, (cols + 2) * frames, lanes), F32),
            pltpu.VMEM((2, slabs, (rows + 2) * pitch + 8, lanes), F32),
            pltpu.VMEM((2, rows * cols, taps * channels), BF16),
            pltpu.SemaphoreType.DMA((2,)),
        ],
        compiler_params=params(),
        cost_estimate=cost(2 * size * channels * taps, 4 * size),
        name="end_frames",
    )(video, left, right, above, below, w_space)


def group_lanes(channels):
    shape = (channels, 128)
    channel = lax.broadcasted_iota(jnp.int32, shape, 0)
    lane = lax.broadcasted_iota(jnp.int32, shape, 1)
    return (channel // (channels // GROUPS) == lane).astype(F32)


def temporal_conv(me, spatial, before, after, w_time):
    pixels, frames, channels = spatial.shape
    parts = lax.axis_size("tm")
    quarter = pixels // parts
    chunk = 16
    count = chunk * frames
    lanes = 128
    slabs = channels // lanes
    pitch = frames + 8
    per_part = quarter // chunk
    steps = parts * per_part

    def kernel(me_ref, s_ref, b_ref, a_ref, w_ref, *rest):
        outs, stats_ref = rest[:parts], rest[parts]
        wides, windows, totals = rest[parts + 1 : parts + 3], rest[parts + 3 : parts + 5], rest[parts + 5 :]

        def base_of(t):
            start = lax.rem(me_ref[0] + t // per_part, parts) * quarter
            return pl.multiple_of(start + (t % per_part) * chunk, chunk)

        def prepare(t):
            base = base_of(t)
            wide, window = wides[t % 2], windows[t % 2]
            x = s_ref[pl.ds(base, chunk)].reshape(count, channels)
            xf = x.astype(F32)
            prev = b_ref[pl.ds(base, chunk)].astype(F32)
            nxt = a_ref[pl.ds(base, chunk)].astype(F32)
            window[:, channels : 2 * channels] = x
            for j in range(slabs):
                cut = slice(j * lanes, (j + 1) * lanes)
                wide[j, pl.ds(7, chunk, stride=pitch)] = prev[:, cut]
                wide[j, pl.ds(pitch, chunk, stride=pitch)] = nxt[:, cut]
                for p in range(chunk):
                    wide[j, pl.ds(p * pitch + 8, frames)] = xf[p * frames : (p + 1) * frames, cut]
            for p in range(chunk):
                for j in range(slabs):
                    for offset, to in ((7, 0), (9, 2)):
                        window[
                            p * frames : (p + 1) * frames,
                            to * channels + j * lanes : to * channels + (j + 1) * lanes,
                        ] = wide[j, pl.ds(p * pitch + offset, frames)].astype(BF16)

        def multiply(t):
            window = windows[t % 2]
            totals[t % 2][...] = jnp.dot(window[...], w_ref[...], preferred_element_type=F32)

        def finish(t, sums):
            x = s_ref[pl.ds(base_of(t), chunk)].reshape(count, channels).astype(F32)
            rounded = (x + totals[t % 2][...]).astype(BF16)
            outs[t // per_part][pl.ds(t % per_part * chunk, chunk)] = rounded.reshape(
                chunk, frames, channels
            )
            kept = rounded.astype(F32).reshape(count // 8, 8, channels)
            return sums[0] + jnp.sum(kept, axis=0), sums[1] + jnp.sum(kept * kept, axis=0)

        sums = (jnp.zeros((8, channels), F32),) * 2
        prepare(0)
        for t in range(steps + 1):
            if t < steps:
                multiply(t)
            if t + 1 < steps:
                prepare(t + 1)
            if t > 0:
                sums = finish(t - 1, sums)
        folded = [jnp.sum(v, axis=0, keepdims=True) for v in sums] + [jnp.zeros((6, channels), F32)]
        stats_ref[...] = jnp.dot(
            jnp.concatenate(folded, axis=0),
            group_lanes(channels),
            precision=lax.Precision.HIGHEST,
            preferred_element_type=F32,
        )

    vmem = pl.BlockSpec(memory_space=pltpu.VMEM)
    size = pixels * frames * channels
    res = pl.pallas_call(
        kernel,
        in_specs=[pl.BlockSpec(memory_space=pltpu.SMEM)] + [vmem] * 4,
        out_specs=[vmem] * (parts + 1),
        out_shape=[jax.ShapeDtypeStruct((quarter, frames, channels), BF16)] * parts
        + [jax.ShapeDtypeStruct((8, 128), F32)],
        scratch_shapes=[pltpu.VMEM((slabs, chunk * pitch + 8, lanes), F32)] * 2
        + [pltpu.VMEM((count, 3 * channels), BF16)] * 2
        + [pltpu.VMEM((count, channels), F32)] * 2,
        compiler_params=params(),
        cost_estimate=cost(2 * size * channels * 3, 4 * size),
        name="temporal_conv",
    )(me, spatial, before, after, w_time.reshape(3 * channels, channels))
    return res[:parts], res[parts]


def attention(blocks, stats, gain, bias, w_qkv, w_out, cell_count, first, pixels):
    parts = len(blocks)
    frames, channels = blocks[0].shape[1:]
    length = parts * frames
    group = 8
    head = channels // HEADS
    half = channels // 2
    per_half = HEADS // 2
    factor = math.log2(math.e) / math.sqrt(head)
    batch = 4

    def kernel(*refs):
        ins, refs = refs[:parts], refs[parts:]
        stats_ref, gain_ref, bias_ref, qkv_ref, out_w_ref = refs[:5]
        outs, refs = refs[5 : 5 + parts], refs[5 + parts :]
        normed, projected, contexts, affine = refs[:2], refs[2:4], refs[4], refs[5]
        spread = lax.dot_general(
            jnp.sum(stats_ref[...], axis=0),
            group_lanes(channels),
            (((1,), (1,)), ((), ())),
            precision=lax.Precision.HIGHEST,
            preferred_element_type=F32,
        )
        mean = spread[0:1] / cell_count
        var = jnp.maximum(spread[1:2] / cell_count - mean * mean, 0.0)
        scale = 0.5 * lax.rsqrt(var + 1e-05) * gain_ref[...]
        affine[0:8] = jnp.broadcast_to(scale, (8, channels))
        affine[8:16] = jnp.broadcast_to(0.5 * bias_ref[...] - mean * scale, (8, channels))
        lane = lax.broadcasted_iota(jnp.int32, (length, channels), 1)
        halves = [(lane // half) == i for i in range(2)]
        heads = [((lane // head) % per_half) == i for i in range(per_half)]

        def normalize(slot, pixel, g):
            x = jnp.concatenate([ref[pixel + g] for ref in ins], axis=0).astype(F32)
            x = x.reshape(length // 8, 8, channels)
            u = (x * affine[0:8][None] + affine[8:16][None]).reshape(length, channels)
            normed[slot][g * length : (g + 1) * length] = (u + u * jnp.tanh(u)).astype(BF16)

        def project(slot, b):
            rows = slice(b * batch * length, (b + 1) * batch * length)
            projected[slot][rows] = jnp.dot(
                normed[slot][rows], qkv_ref[...], preferred_element_type=F32
            ).astype(BF16)

        zero = jnp.zeros((length, channels), BF16)

        def score(slot, g):
            rows = slice(g * length, (g + 1) * length)
            q = projected[slot][rows, :channels]
            k = projected[slot][rows, channels : 2 * channels]
            qm = jnp.concatenate([jnp.where(m, q, zero) for m in halves], axis=0)
            km = jnp.concatenate([jnp.where(m, k, zero) for m in heads], axis=0)
            return lax.dot_general(
                km, qm, (((1,), (1,)), ((), ())), preferred_element_type=F32
            ).reshape(per_half, length, 2 * length)

        def soften(scores):
            top = jnp.max(scores, axis=1, keepdims=True)
            e = jnp.exp2((scores - top) * factor)
            weights = (e * (1.0 / jnp.sum(e, axis=1, keepdims=True))).astype(BF16)
            return weights.reshape(per_half * length, 2 * length)

        def mix(slot, g, weights):
            rows = slice(g * length, (g + 1) * length)
            val = projected[slot][rows, 2 * channels :]
            vm = jnp.concatenate([jnp.where(m, val, zero) for m in heads], axis=0)
            mixed = lax.dot_general(
                weights, vm, (((0,), (0,)), ((), ())), preferred_element_type=F32
            )
            contexts[rows] = jnp.concatenate(
                [mixed[:length, :half], mixed[length:, half:]], axis=1
            ).astype(BF16)

        def finish(slot, pixel, b):
            rows = slice(b * batch * length, (b + 1) * batch * length)
            result = normed[slot][rows].astype(F32) + jnp.dot(
                contexts[rows], out_w_ref[...], preferred_element_type=F32
            )
            result = result.astype(BF16).reshape(batch, parts, frames, channels)
            for d in range(parts):
                outs[d][pl.ds(pixel - first + b * batch, batch)] = result[:, d]

        def work(slot, pixel, ahead):
            scores, weights = {}, {}
            for t in range(group + 2):
                if t < group:
                    scores[t] = score(slot, t)
                    normalize(1 - slot, ahead, t)
                    if (t + 1) % batch == 0:
                        project(1 - slot, t // batch)
                if 0 <= t - 1 < group:
                    weights[t - 1] = soften(scores.pop(t - 1))
                if 0 <= t - 2 < group:
                    mix(slot, t - 2, weights.pop(t - 2))
                    if (t - 1) % batch == 0:
                        finish(slot, pixel, (t - 2) // batch)

        for g in range(group):
            normalize(0, first, g)
        for b in range(group // batch):
            project(0, b)

        def body(i, carry):
            pixel = first + i * 2 * group
            work(0, pixel, pixel + group)
            ahead = jnp.minimum(pixel + 2 * group, first + pixels - group)
            work(1, pixel + group, ahead)
            return carry

        lax.fori_loop(0, pixels // (2 * group), body, 0)

    rest = (stats, gain, bias, w_qkv, w_out)
    vmem = pl.BlockSpec(memory_space=pltpu.VMEM)
    size = parts * pixels * frames * channels
    return pl.pallas_call(
        kernel,
        in_specs=[vmem] * (parts + len(rest)),
        out_specs=[vmem] * parts,
        out_shape=[jax.ShapeDtypeStruct((pixels, frames, channels), BF16)] * parts,
        scratch_shapes=[pltpu.VMEM((group * length, channels), BF16)] * 2
        + [pltpu.VMEM((group * length, 3 * channels), BF16)] * 2
        + [pltpu.VMEM((group * length, channels), BF16), pltpu.VMEM((16, channels), F32)],
        compiler_params=params(),
        cost_estimate=cost(2 * size * channels * 8, 4 * size, size * 3),
        name="attention",
    )(*blocks, *rest)


def from_pixels(me, blocks, moves, shape, result=None):
    frames, rows, cols, channels = shape
    parts = lax.axis_size("tm")
    half_rows = blocks[0].shape[0] // cols
    part_rows = rows // parts
    total = len(blocks) * half_rows
    given = [] if result is None else [result]

    def kernel(me_ref, *refs):
        ins, out_ref, turned, sem = refs[: len(blocks)], refs[-3], refs[-2], refs[-1]
        copies = []
        for n, (d, h) in enumerate(moves):
            base = lax.rem(me_ref[0] + d, parts) * part_rows + h * half_rows
            for r in range(half_rows):
                slot = len(copies)
                turned[slot] = jnp.swapaxes(ins[n][pl.ds(r * cols, cols)], 0, 1)
                copy = pltpu.make_async_copy(turned.at[slot], out_ref.at[:, base + r], sem.at[slot])
                copy.start()
                copies.append(copy)
        for copy in copies:
            copy.wait()

    vmem = pl.BlockSpec(memory_space=pltpu.VMEM)
    anywhere = pl.BlockSpec(memory_space=pl.ANY)
    return pl.pallas_call(
        kernel,
        in_specs=[pl.BlockSpec(memory_space=pltpu.SMEM)]
        + [vmem] * len(blocks)
        + [anywhere] * len(given),
        out_specs=anywhere,
        out_shape=jax.ShapeDtypeStruct(shape, BF16),
        input_output_aliases={1 + len(blocks): 0} if given else {},
        scratch_shapes=[
            pltpu.VMEM((total, frames, cols, channels), BF16),
            pltpu.SemaphoreType.DMA((total,)),
        ],
        compiler_params=params(),
        cost_estimate=cost(0, 4 * total * frames * cols * channels),
        name="from_pixels",
    )(me, *blocks, *given)


def rotate(value, step):
    size = lax.axis_size("tm")
    return lax.ppermute(value, "tm", [(i, (i + step) % size) for i in range(size)])


def per_device(video, w_space, w_time, norm_gain, norm_bias, w_qkv, w_out):
    frames, rows, cols, channels = video.shape
    parts = lax.axis_size("tm")
    me = lax.axis_index("tm").astype(jnp.int32).reshape(1)
    left = shift(jnp.swapaxes(video[:, :, cols - 1], 0, 1), WIDTH, 1)
    right = shift(jnp.swapaxes(video[:, :, 0], 0, 1), WIDTH, -1)
    pixels = to_pixels(video)

    def border(r):
        return jnp.concatenate([left[r][None], pixels[r], right[r][None]], axis=0)

    above = shift(border(rows - 1), "height", 1)
    below = shift(border(0), "height", -1)
    taps = w_space.reshape(9 * channels, channels)
    early, late = end_frames(video, left, right, above, below, taps)
    before = shift(late, "tm", 1)
    after = shift(early, "tm", -1)
    spatial = spatial_conv(pixels, left, right, above, below, taps)
    blocks, stats = temporal_conv(
        me, spatial.reshape(rows * cols, frames, channels), before, after, w_time
    )
    stats = stats + sum(rotate(stats, d) for d in range(1, parts))
    moved = [blocks[0]]
    for d in range(1, parts):
        moved.append(rotate(blocks[d], d))
    stats = stats + lax.ppermute(stats, "width_1", [(0, 1), (1, 0)])
    others = ("height", "width_0")
    count = lax.axis_size(others)
    shared = jnp.broadcast_to(stats[None], (count, *stats.shape))
    stats = lax.all_to_all(shared, others, 0, 0)
    cell_count = float(
        frames * parts * rows * lax.axis_size("height") * cols * lax.axis_size(WIDTH)
        * (channels // GROUPS)
    )
    weights = (norm_gain.reshape(1, -1), norm_bias.reshape(1, -1), w_qkv, w_out)
    share = rows * cols // parts // 2
    own, far = [], []
    for h in range(2):
        results = attention(moved, stats, *weights, cell_count, h * share, share)
        own.append(results[0])
        far.append([rotate(results[d], -d) for d in range(1, parts)])
    moves = [(0, 0), (0, 1)] + [(d, 0) for d in range(1, parts)]
    result = from_pixels(me, own + far[0], moves, video.shape)
    return from_pixels(me, far[1], [(d, 1) for d in range(1, parts)], video.shape, result)


def solution(mesh):
    torus = Mesh(
        mesh.devices.reshape(mesh.shape["tm"], mesh.shape["height"], 8, 2),
        ("tm", "height", "width_0", "width_1"),
    )
    in_specs = (P("tm", "height", WIDTH, None), P(), P(), P(), P(), P(), P())
    out_specs = P("tm", "height", WIDTH, None)
    return jax.shard_map(
        per_device, mesh=torus, in_specs=in_specs, out_specs=out_specs, check_vma=False
    )
```

```python
import math

import jax
import jax.numpy as jnp
from jax import lax
from jax.experimental import pallas as pl
from jax.experimental.pallas import tpu as pltpu
from jax.sharding import Mesh
from jax.sharding import PartitionSpec as P

HEADS = 8
GROUPS = 32
WIDTH = ("width_0", "width_1")
BF16 = jnp.bfloat16
F32 = jnp.float32
VMEM_BYTES = 16 * 1024 * 1024


def params(**kw):
    return pltpu.CompilerParams(vmem_limit_bytes=VMEM_BYTES, **kw)


def cost(flops, nbytes, trans=0):
    return pl.CostEstimate(flops=flops, bytes_accessed=nbytes, transcendentals=trans)


def shift(value, axis, step):
    size = lax.axis_size(axis)
    if step > 0:
        pairs = [(i, i + 1) for i in range(size - 1)]
    else:
        pairs = [(i + 1, i) for i in range(size - 1)]
    return lax.ppermute(value, axis, pairs)


def edge_columns(video):
    frames, rows, cols, channels = video.shape

    def kernel(v_ref, first_ref, last_ref):
        for r in range(rows):
            turned = jnp.swapaxes(v_ref[:, r], 0, 1)
            first_ref[r] = turned[0]
            last_ref[r] = turned[cols - 1]

    return pl.pallas_call(
        kernel,
        out_shape=[jax.ShapeDtypeStruct((rows, frames, channels), BF16)] * 2,
        compiler_params=params(),
        cost_estimate=cost(0, video.size * 2),
        name="edge_columns",
    )(video)


def extend_columns(first, last, above, below):
    rows, frames, channels = first.shape
    cols = above.shape[1]

    def kernel(f_ref, l_ref, a_ref, b_ref, *outs):
        for ref, row in ((a_ref, 0), (b_ref, rows + 1)):
            turned = jnp.swapaxes(ref[...], 0, 1)
            outs[0][row] = turned[0]
            outs[1][row] = turned[cols - 1]
        for out, ref in zip(outs, (f_ref, l_ref)):
            out[pl.ds(1, rows)] = ref[...]

    return pl.pallas_call(
        kernel,
        out_shape=[jax.ShapeDtypeStruct((rows + 2, frames, channels), BF16)] * 2,
        compiler_params=params(),
        cost_estimate=cost(0, 8 * first.size),
        name="extend_columns",
    )(first, last, above, below)


def spatial_conv(video, above, below, left, right, w_space):
    frames, rows, cols, channels = video.shape
    span = 2
    count = span * cols * frames
    unroll = 2

    def kernel(v_ref, a_ref, b_ref, l_ref, r_ref, w_ref, out_ref, pad):
        for r in range(rows + 2):
            row = a_ref[...] if r == 0 else b_ref[...] if r == rows + 1 else v_ref[:, r - 1]
            pad[r, 0] = l_ref[r]
            pad[r, pl.ds(1, cols)] = jnp.swapaxes(row, 0, 1)
            pad[r, cols + 1] = r_ref[r]

        def body(i, carry):
            for u in range(unroll):
                base = (i * unroll + u) * span
                pieces = []
                for row_step in range(3):
                    for col_step in range(3):
                        piece = pad[pl.ds(base + row_step, span), pl.ds(col_step, cols)]
                        pieces.append(piece.reshape(count, channels))
                window = jnp.concatenate(pieces, axis=1)
                total = jnp.dot(window, w_ref[...], preferred_element_type=F32)
                out_ref[pl.ds(base, span)] = total.astype(BF16).reshape(
                    span, cols, frames, channels
                )
            return carry

        lax.fori_loop(0, rows // span // unroll, body, 0)

    size = rows * cols * frames * channels
    return pl.pallas_call(
        kernel,
        out_shape=jax.ShapeDtypeStruct((rows, cols, frames, channels), BF16),
        scratch_shapes=[pltpu.VMEM((rows + 2, cols + 2, frames, channels), BF16)],
        compiler_params=params(),
        cost_estimate=cost(2 * size * channels * 9, 4 * size),
        name="spatial_conv",
    )(video, above, below, left, right, w_space)


def end_frames(video, above, below, left, right, w_space):
    frames, rows, cols, channels = video.shape
    lanes = 128
    slabs = channels // lanes
    pitch = cols + 8
    taps = 9
    ends = (0, frames - 1)

    def kernel(v_ref, a_ref, b_ref, l_ref, r_ref, w_ref, early_ref, late_ref, held, side, wide, window, sem):
        fetch = [
            pltpu.make_async_copy(v_ref.at[frame], held.at[k], sem.at[k])
            for k, frame in enumerate(ends)
        ]
        for copy in fetch:
            copy.start()
        for j in range(slabs):
            cut = slice(j * lanes, (j + 1) * lanes)
            for n, ref in enumerate((l_ref, r_ref)):
                size = (rows + 2) * frames
                side[n, j] = ref[...].reshape(size, channels)[:, cut].astype(F32)
        for copy in fetch:
            copy.wait()
        outs = (early_ref, late_ref)
        for k, frame in enumerate(ends):
            for j in range(slabs):
                cut = slice(j * lanes, (j + 1) * lanes)
                for n, at in ((0, 7), (1, pitch)):
                    wide[k, j, pl.ds(at, rows + 2, stride=pitch)] = side[
                        n, j, pl.ds(frame, rows + 2, stride=frames)
                    ]
                for ref, row in ((a_ref, 0), (b_ref, rows + 1)):
                    wide[k, j, pl.ds(row * pitch + 8, cols)] = ref[frame, :, cut].astype(F32)
                for r in range(rows):
                    wide[k, j, pl.ds((r + 1) * pitch + 8, cols)] = held[k, r, :, cut].astype(F32)
            for tap in range(taps):
                row_step, col_step = tap // 3, tap % 3
                for r in range(rows):
                    for j in range(slabs):
                        at = tap * channels + j * lanes
                        window[k, r * cols : (r + 1) * cols, at : at + lanes] = wide[
                            k, j, pl.ds((r + row_step) * pitch + 7 + col_step, cols)
                        ].astype(BF16)
            outs[k][...] = jnp.dot(
                window[k], w_ref[...], preferred_element_type=F32
            ).astype(BF16)

    anywhere = pl.BlockSpec(memory_space=pl.ANY)
    vmem = pl.BlockSpec(memory_space=pltpu.VMEM)
    size = 2 * rows * cols * channels
    return pl.pallas_call(
        kernel,
        in_specs=[anywhere] + [vmem] * 5,
        out_specs=[vmem] * 2,
        out_shape=[jax.ShapeDtypeStruct((rows * cols, channels), BF16)] * 2,
        scratch_shapes=[
            pltpu.VMEM((2, rows, cols, channels), BF16),
            pltpu.VMEM((2, slabs, (rows + 2) * frames, lanes), F32),
            pltpu.VMEM((2, slabs, (rows + 2) * pitch + 8, lanes), F32),
            pltpu.VMEM((2, rows * cols, taps * channels), BF16),
            pltpu.SemaphoreType.DMA((2,)),
        ],
        compiler_params=params(),
        cost_estimate=cost(2 * size * channels * taps, 4 * size),
        name="end_frames",
    )(video, above, below, left, right, w_space)


def group_lanes(channels):
    shape = (channels, 128)
    channel = lax.broadcasted_iota(jnp.int32, shape, 0)
    lane = lax.broadcasted_iota(jnp.int32, shape, 1)
    return (channel // (channels // GROUPS) == lane).astype(F32)


def temporal_conv(me, spatial, before, after, w_time):
    pixels, frames, channels = spatial.shape
    parts = lax.axis_size("tm")
    quarter = pixels // parts
    chunk = 16
    count = chunk * frames
    lanes = 128
    slabs = channels // lanes
    pitch = frames + 8
    per_part = quarter // chunk
    steps = parts * per_part

    def kernel(me_ref, s_ref, b_ref, a_ref, w_ref, *rest):
        outs, stats_ref = rest[:parts], rest[parts]
        wides, windows, totals = rest[parts + 1 : parts + 3], rest[parts + 3 : parts + 5], rest[parts + 5 :]

        def base_of(t):
            start = lax.rem(me_ref[0] + t // per_part, parts) * quarter
            return pl.multiple_of(start + (t % per_part) * chunk, chunk)

        def prepare(t):
            base = base_of(t)
            wide, window = wides[t % 2], windows[t % 2]
            x = s_ref[pl.ds(base, chunk)].reshape(count, channels)
            xf = x.astype(F32)
            prev = b_ref[pl.ds(base, chunk)].astype(F32)
            nxt = a_ref[pl.ds(base, chunk)].astype(F32)
            window[:, channels : 2 * channels] = x
            for j in range(slabs):
                cut = slice(j * lanes, (j + 1) * lanes)
                wide[j, pl.ds(7, chunk, stride=pitch)] = prev[:, cut]
                wide[j, pl.ds(pitch, chunk, stride=pitch)] = nxt[:, cut]
                for p in range(chunk):
                    wide[j, pl.ds(p * pitch + 8, frames)] = xf[p * frames : (p + 1) * frames, cut]
            for p in range(chunk):
                for j in range(slabs):
                    for offset, to in ((7, 0), (9, 2)):
                        window[
                            p * frames : (p + 1) * frames,
                            to * channels + j * lanes : to * channels + (j + 1) * lanes,
                        ] = wide[j, pl.ds(p * pitch + offset, frames)].astype(BF16)

        def multiply(t):
            window = windows[t % 2]
            totals[t % 2][...] = jnp.dot(window[...], w_ref[...], preferred_element_type=F32)

        def finish(t, sums):
            x = s_ref[pl.ds(base_of(t), chunk)].reshape(count, channels).astype(F32)
            rounded = (x + totals[t % 2][...]).astype(BF16)
            outs[t // per_part][pl.ds(t % per_part * chunk, chunk)] = rounded.reshape(
                chunk, frames, channels
            )
            kept = rounded.astype(F32).reshape(count // 8, 8, channels)
            return sums[0] + jnp.sum(kept, axis=0), sums[1] + jnp.sum(kept * kept, axis=0)

        sums = (jnp.zeros((8, channels), F32),) * 2
        prepare(0)
        for t in range(steps + 1):
            if t < steps:
                multiply(t)
            if t + 1 < steps:
                prepare(t + 1)
            if t > 0:
                sums = finish(t - 1, sums)
        folded = [jnp.sum(v, axis=0, keepdims=True) for v in sums] + [jnp.zeros((6, channels), F32)]
        stats_ref[...] = jnp.dot(
            jnp.concatenate(folded, axis=0),
            group_lanes(channels),
            precision=lax.Precision.HIGHEST,
            preferred_element_type=F32,
        )

    vmem = pl.BlockSpec(memory_space=pltpu.VMEM)
    size = pixels * frames * channels
    res = pl.pallas_call(
        kernel,
        in_specs=[pl.BlockSpec(memory_space=pltpu.SMEM)] + [vmem] * 4,
        out_specs=[vmem] * (parts + 1),
        out_shape=[jax.ShapeDtypeStruct((quarter, frames, channels), BF16)] * parts
        + [jax.ShapeDtypeStruct((8, 128), F32)],
        scratch_shapes=[pltpu.VMEM((slabs, chunk * pitch + 8, lanes), F32)] * 2
        + [pltpu.VMEM((count, 3 * channels), BF16)] * 2
        + [pltpu.VMEM((count, channels), F32)] * 2,
        compiler_params=params(),
        cost_estimate=cost(2 * size * channels * 3, 4 * size),
        name="temporal_conv",
    )(me, spatial, before, after, w_time.reshape(3 * channels, channels))
    return res[:parts], res[parts]


def attention(blocks, stats, gain, bias, w_qkv, w_out, cell_count, first, pixels):
    parts = len(blocks)
    frames, channels = blocks[0].shape[1:]
    length = parts * frames
    group = 8
    head = channels // HEADS
    half = channels // 2
    per_half = HEADS // 2
    factor = math.log2(math.e) / math.sqrt(head)
    batch = 4

    def kernel(*refs):
        ins, refs = refs[:parts], refs[parts:]
        stats_ref, gain_ref, bias_ref, qkv_ref, out_w_ref = refs[:5]
        outs, refs = refs[5 : 5 + parts], refs[5 + parts :]
        normed, projected, contexts, affine = refs[:2], refs[2:4], refs[4], refs[5]
        spread = lax.dot_general(
            jnp.sum(stats_ref[...], axis=0),
            group_lanes(channels),
            (((1,), (1,)), ((), ())),
            precision=lax.Precision.HIGHEST,
            preferred_element_type=F32,
        )
        mean = spread[0:1] / cell_count
        var = jnp.maximum(spread[1:2] / cell_count - mean * mean, 0.0)
        scale = 0.5 * lax.rsqrt(var + 1e-05) * gain_ref[...]
        affine[0:8] = jnp.broadcast_to(scale, (8, channels))
        affine[8:16] = jnp.broadcast_to(0.5 * bias_ref[...] - mean * scale, (8, channels))
        lane = lax.broadcasted_iota(jnp.int32, (length, channels), 1)
        halves = [(lane // half) == i for i in range(2)]
        heads = [((lane // head) % per_half) == i for i in range(per_half)]

        def normalize(slot, pixel, g):
            x = jnp.concatenate([ref[pixel + g] for ref in ins], axis=0).astype(F32)
            x = x.reshape(length // 8, 8, channels)
            u = (x * affine[0:8][None] + affine[8:16][None]).reshape(length, channels)
            normed[slot][g * length : (g + 1) * length] = (u + u * jnp.tanh(u)).astype(BF16)

        def project(slot, b):
            rows = slice(b * batch * length, (b + 1) * batch * length)
            projected[slot][rows] = jnp.dot(
                normed[slot][rows], qkv_ref[...], preferred_element_type=F32
            ).astype(BF16)

        zero = jnp.zeros((length, channels), BF16)

        def score(slot, g):
            rows = slice(g * length, (g + 1) * length)
            q = projected[slot][rows, :channels]
            k = projected[slot][rows, channels : 2 * channels]
            qm = jnp.concatenate([jnp.where(m, q, zero) for m in halves], axis=0)
            km = jnp.concatenate([jnp.where(m, k, zero) for m in heads], axis=0)
            return lax.dot_general(
                km, qm, (((1,), (1,)), ((), ())), preferred_element_type=F32
            ).reshape(per_half, length, 2 * length)

        def soften(scores):
            top = jnp.max(scores, axis=1, keepdims=True)
            e = jnp.exp2((scores - top) * factor)
            weights = (e * (1.0 / jnp.sum(e, axis=1, keepdims=True))).astype(BF16)
            return weights.reshape(per_half * length, 2 * length)

        def mix(slot, g, weights):
            rows = slice(g * length, (g + 1) * length)
            val = projected[slot][rows, 2 * channels :]
            vm = jnp.concatenate([jnp.where(m, val, zero) for m in heads], axis=0)
            mixed = lax.dot_general(
                weights, vm, (((0,), (0,)), ((), ())), preferred_element_type=F32
            )
            contexts[rows] = jnp.concatenate(
                [mixed[:length, :half], mixed[length:, half:]], axis=1
            ).astype(BF16)

        def finish(slot, pixel, b):
            rows = slice(b * batch * length, (b + 1) * batch * length)
            result = normed[slot][rows].astype(F32) + jnp.dot(
                contexts[rows], out_w_ref[...], preferred_element_type=F32
            )
            result = result.astype(BF16).reshape(batch, parts, frames, channels)
            for d in range(parts):
                outs[d][pl.ds(pixel - first + b * batch, batch)] = result[:, d]

        def work(slot, pixel, ahead):
            scores, weights = {}, {}
            for t in range(group + 2):
                if t < group:
                    scores[t] = score(slot, t)
                    normalize(1 - slot, ahead, t)
                    if (t + 1) % batch == 0:
                        project(1 - slot, t // batch)
                if 0 <= t - 1 < group:
                    weights[t - 1] = soften(scores.pop(t - 1))
                if 0 <= t - 2 < group:
                    mix(slot, t - 2, weights.pop(t - 2))
                    if (t - 1) % batch == 0:
                        finish(slot, pixel, (t - 2) // batch)

        for g in range(group):
            normalize(0, first, g)
        for b in range(group // batch):
            project(0, b)

        def body(i, carry):
            pixel = first + i * 2 * group
            work(0, pixel, pixel + group)
            ahead = jnp.minimum(pixel + 2 * group, first + pixels - group)
            work(1, pixel + group, ahead)
            return carry

        lax.fori_loop(0, pixels // (2 * group), body, 0)

    rest = (stats, gain, bias, w_qkv, w_out)
    vmem = pl.BlockSpec(memory_space=pltpu.VMEM)
    size = parts * pixels * frames * channels
    return pl.pallas_call(
        kernel,
        in_specs=[vmem] * (parts + len(rest)),
        out_specs=[vmem] * parts,
        out_shape=[jax.ShapeDtypeStruct((pixels, frames, channels), BF16)] * parts,
        scratch_shapes=[pltpu.VMEM((group * length, channels), BF16)] * 2
        + [pltpu.VMEM((group * length, 3 * channels), BF16)] * 2
        + [pltpu.VMEM((group * length, channels), BF16), pltpu.VMEM((16, channels), F32)],
        compiler_params=params(),
        cost_estimate=cost(2 * size * channels * 8, 4 * size, size * 3),
        name="attention",
    )(*blocks, *rest)


def from_pixels(me, blocks, moves, shape, result=None):
    frames, rows, cols, channels = shape
    parts = lax.axis_size("tm")
    half_rows = blocks[0].shape[0] // cols
    part_rows = rows // parts
    total = len(blocks) * half_rows
    given = [] if result is None else [result]

    def kernel(me_ref, *refs):
        ins, out_ref, turned, sem = refs[: len(blocks)], refs[-3], refs[-2], refs[-1]
        copies = []
        for n, (d, h) in enumerate(moves):
            base = lax.rem(me_ref[0] + d, parts) * part_rows + h * half_rows
            for r in range(half_rows):
                slot = len(copies)
                turned[slot] = jnp.swapaxes(ins[n][pl.ds(r * cols, cols)], 0, 1)
                copy = pltpu.make_async_copy(turned.at[slot], out_ref.at[:, base + r], sem.at[slot])
                copy.start()
                copies.append(copy)
        for copy in copies:
            copy.wait()

    vmem = pl.BlockSpec(memory_space=pltpu.VMEM)
    anywhere = pl.BlockSpec(memory_space=pl.ANY)
    return pl.pallas_call(
        kernel,
        in_specs=[pl.BlockSpec(memory_space=pltpu.SMEM)]
        + [vmem] * len(blocks)
        + [anywhere] * len(given),
        out_specs=anywhere,
        out_shape=jax.ShapeDtypeStruct(shape, BF16),
        input_output_aliases={1 + len(blocks): 0} if given else {},
        scratch_shapes=[
            pltpu.VMEM((total, frames, cols, channels), BF16),
            pltpu.SemaphoreType.DMA((total,)),
        ],
        compiler_params=params(),
        cost_estimate=cost(0, 4 * total * frames * cols * channels),
        name="from_pixels",
    )(me, *blocks, *given)


def rotate(value, step):
    size = lax.axis_size("tm")
    return lax.ppermute(value, "tm", [(i, (i + step) % size) for i in range(size)])


def per_device(video, w_space, w_time, norm_gain, norm_bias, w_qkv, w_out):
    frames, rows, cols, channels = video.shape
    parts = lax.axis_size("tm")
    me = lax.axis_index("tm").astype(jnp.int32).reshape(1)
    above = shift(video[:, rows - 1], "height", 1)
    below = shift(video[:, 0], "height", -1)
    first, last = extend_columns(*edge_columns(video), above, below)
    left = shift(last, WIDTH, 1)
    right = shift(first, WIDTH, -1)
    taps = w_space.reshape(9 * channels, channels)
    early, late = end_frames(video, above, below, left, right, taps)
    before = shift(late, "tm", 1)
    after = shift(early, "tm", -1)
    spatial = spatial_conv(video, above, below, left, right, taps)
    blocks, stats = temporal_conv(
        me, spatial.reshape(rows * cols, frames, channels), before, after, w_time
    )
    stats = stats + sum(rotate(stats, d) for d in range(1, parts))
    moved = [blocks[0]]
    for d in range(1, parts):
        moved.append(rotate(blocks[d], d))
    stats = stats + lax.ppermute(stats, "width_1", [(0, 1), (1, 0)])
    others = ("height", "width_0")
    count = lax.axis_size(others)
    shared = jnp.broadcast_to(stats[None], (count, *stats.shape))
    stats = lax.all_to_all(shared, others, 0, 0)
    cell_count = float(
        frames * parts * rows * lax.axis_size("height") * cols * lax.axis_size(WIDTH)
        * (channels // GROUPS)
    )
    weights = (norm_gain.reshape(1, -1), norm_bias.reshape(1, -1), w_qkv, w_out)
    share = rows * cols // parts // 2
    own, far = [], []
    for h in range(2):
        results = attention(moved, stats, *weights, cell_count, h * share, share)
        own.append(results[0])
        far.append([rotate(results[d], -d) for d in range(1, parts)])
    moves = [(0, 0), (0, 1)] + [(d, 0) for d in range(1, parts)]
    result = from_pixels(me, own + far[0], moves, video.shape)
    return from_pixels(me, far[1], [(d, 1) for d in range(1, parts)], video.shape, result)


def solution(mesh):
    torus = Mesh(
        mesh.devices.reshape(mesh.shape["tm"], mesh.shape["height"], 8, 2),
        ("tm", "height", "width_0", "width_1"),
    )
    in_specs = (P("tm", "height", WIDTH, None), P(), P(), P(), P(), P(), P())
    out_specs = P("tm", "height", WIDTH, None)
    return jax.shard_map(
        per_device, mesh=torus, in_specs=in_specs, out_specs=out_specs, check_vma=False
    )
```

```python
import math

import jax
import jax.numpy as jnp
from jax import lax
from jax.experimental import pallas as pl
from jax.experimental.pallas import tpu as pltpu
from jax.sharding import Mesh
from jax.sharding import PartitionSpec as P

HEADS = 8
GROUPS = 32
WIDTH = ("width_0", "width_1")
BF16 = jnp.bfloat16
F32 = jnp.float32
VMEM_BYTES = 16 * 1024 * 1024


def params(**kw):
    return pltpu.CompilerParams(vmem_limit_bytes=VMEM_BYTES, **kw)


def cost(flops, nbytes, trans=0):
    return pl.CostEstimate(flops=flops, bytes_accessed=nbytes, transcendentals=trans)


def shift(value, axis, step):
    size = lax.axis_size(axis)
    if step > 0:
        pairs = [(i, i + 1) for i in range(size - 1)]
    else:
        pairs = [(i + 1, i) for i in range(size - 1)]
    return lax.ppermute(value, axis, pairs)


def edge_columns(video):
    frames, rows, cols, channels = video.shape

    def kernel(v_ref, first_ref, last_ref):
        for r in range(rows):
            turned = jnp.swapaxes(v_ref[:, r], 0, 1)
            first_ref[r] = turned[0]
            last_ref[r] = turned[cols - 1]

    return pl.pallas_call(
        kernel,
        out_shape=[jax.ShapeDtypeStruct((rows, frames, channels), BF16)] * 2,
        compiler_params=params(),
        cost_estimate=cost(0, video.size * 2),
        name="edge_columns",
    )(video)


def extend_columns(first, last, above, below):
    rows, frames, channels = first.shape
    cols = above.shape[1]

    def kernel(f_ref, l_ref, a_ref, b_ref, *outs):
        for ref, row in ((a_ref, 0), (b_ref, rows + 1)):
            turned = jnp.swapaxes(ref[...], 0, 1)
            outs[0][row] = turned[0]
            outs[1][row] = turned[cols - 1]
        for out, ref in zip(outs, (f_ref, l_ref)):
            out[pl.ds(1, rows)] = ref[...]

    return pl.pallas_call(
        kernel,
        out_shape=[jax.ShapeDtypeStruct((rows + 2, frames, channels), BF16)] * 2,
        compiler_params=params(),
        cost_estimate=cost(0, 8 * first.size),
        name="extend_columns",
    )(first, last, above, below)


def spatial_conv(video, above, below, left, right, w_space):
    frames, rows, cols, channels = video.shape
    span = 2
    count = span * cols * frames
    unroll = 2

    def kernel(v_ref, a_ref, b_ref, l_ref, r_ref, w_ref, out_ref, pad):
        for r in range(rows + 2):
            row = a_ref[...] if r == 0 else b_ref[...] if r == rows + 1 else v_ref[:, r - 1]
            pad[r, 0] = l_ref[r]
            pad[r, pl.ds(1, cols)] = jnp.swapaxes(row, 0, 1)
            pad[r, cols + 1] = r_ref[r]

        def body(i, carry):
            for u in range(unroll):
                base = (i * unroll + u) * span
                pieces = []
                for row_step in range(3):
                    for col_step in range(3):
                        piece = pad[pl.ds(base + row_step, span), pl.ds(col_step, cols)]
                        pieces.append(piece.reshape(count, channels))
                window = jnp.concatenate(pieces, axis=1)
                total = jnp.dot(window, w_ref[...], preferred_element_type=F32)
                out_ref[pl.ds(base, span)] = total.astype(BF16).reshape(
                    span, cols, frames, channels
                )
            return carry

        lax.fori_loop(0, rows // span // unroll, body, 0)

    size = rows * cols * frames * channels
    return pl.pallas_call(
        kernel,
        out_shape=jax.ShapeDtypeStruct((rows, cols, frames, channels), BF16),
        scratch_shapes=[pltpu.VMEM((rows + 2, cols + 2, frames, channels), BF16)],
        compiler_params=params(),
        cost_estimate=cost(2 * size * channels * 9, 4 * size),
        name="spatial_conv",
    )(video, above, below, left, right, w_space)


def end_frames(video, above, below, left, right, w_space):
    frames, rows, cols, channels = video.shape
    lanes = 128
    slabs = channels // lanes
    pitch = cols + 8
    taps = 9
    ends = (0, frames - 1)
    whole_rows = -(-(rows + 2) // 8) * 8

    def kernel(v_ref, a_ref, b_ref, l_ref, r_ref, w_ref, early_ref, late_ref, held, side, wide, window, sem):
        fetch = [
            pltpu.make_async_copy(v_ref.at[frame], held.at[k], sem.at[k])
            for k, frame in enumerate(ends)
        ]
        for copy in fetch:
            copy.start()
        for j in range(slabs):
            cut = slice(j * lanes, (j + 1) * lanes)
            for n, ref in enumerate((l_ref, r_ref)):
                size = (rows + 2) * frames
                side[n, j, pl.ds(0, size)] = ref[...].reshape(size, channels)[:, cut].astype(F32)
        for copy in fetch:
            copy.wait()
        outs = (early_ref, late_ref)
        for k, frame in enumerate(ends):
            for j in range(slabs):
                cut = slice(j * lanes, (j + 1) * lanes)
                for n, at in ((0, 7), (1, pitch)):
                    wide[k, j, pl.ds(at, rows + 2, stride=pitch)] = side[
                        n, j, pl.ds(frame, rows + 2, stride=frames)
                    ]
                for ref, row in ((a_ref, 0), (b_ref, rows + 1)):
                    wide[k, j, pl.ds(row * pitch + 8, cols)] = ref[frame, :, cut].astype(F32)
                for r in range(rows):
                    wide[k, j, pl.ds((r + 1) * pitch + 8, cols)] = held[k, r, :, cut].astype(F32)
            for tap in range(taps):
                row_step, col_step = tap // 3, tap % 3
                for r in range(rows):
                    for j in range(slabs):
                        at = tap * channels + j * lanes
                        window[k, r * cols : (r + 1) * cols, at : at + lanes] = wide[
                            k, j, pl.ds((r + row_step) * pitch + 7 + col_step, cols)
                        ].astype(BF16)
            outs[k][...] = jnp.dot(
                window[k], w_ref[...], preferred_element_type=F32
            ).astype(BF16)

    anywhere = pl.BlockSpec(memory_space=pl.ANY)
    vmem = pl.BlockSpec(memory_space=pltpu.VMEM)
    size = 2 * rows * cols * channels
    return pl.pallas_call(
        kernel,
        in_specs=[anywhere] + [vmem] * 5,
        out_specs=[vmem] * 2,
        out_shape=[jax.ShapeDtypeStruct((rows * cols, channels), BF16)] * 2,
        scratch_shapes=[
            pltpu.VMEM((2, rows, cols, channels), BF16),
            pltpu.VMEM((2, slabs, whole_rows * frames, lanes), F32),
            pltpu.VMEM((2, slabs, (whole_rows + 1) * pitch, lanes), F32),
            pltpu.VMEM((2, rows * cols, taps * channels), BF16),
            pltpu.SemaphoreType.DMA((2,)),
        ],
        compiler_params=params(),
        cost_estimate=cost(2 * size * channels * taps, 4 * size),
        name="end_frames",
    )(video, above, below, left, right, w_space)


def group_lanes(channels, first):
    shape = (channels, 128)
    channel = lax.broadcasted_iota(jnp.int32, shape, 0)
    lane = lax.broadcasted_iota(jnp.int32, shape, 1)
    return (channel // (channels // GROUPS) + first == lane).astype(F32)


def temporal_conv(me, spatial, before, after, w_time):
    pixels, frames, channels = spatial.shape
    parts = lax.axis_size("tm")
    quarter = pixels // parts
    chunk = 16
    count = chunk * frames
    lanes = 128
    slabs = channels // lanes
    pitch = frames + 8
    per_part = quarter // chunk
    steps = parts * per_part

    def kernel(me_ref, s_ref, b_ref, a_ref, w_ref, *rest):
        outs, stats_ref = rest[:parts], rest[parts]
        wides, windows, totals = rest[parts + 1 : parts + 3], rest[parts + 3 : parts + 5], rest[parts + 5 :]

        def base_of(t):
            start = lax.rem(me_ref[0] + t // per_part, parts) * quarter
            return pl.multiple_of(start + (t % per_part) * chunk, chunk)

        def prepare(t):
            base = base_of(t)
            wide, window = wides[t % 2], windows[t % 2]
            x = s_ref[pl.ds(base, chunk)].reshape(count, channels)
            xf = x.astype(F32)
            prev = b_ref[pl.ds(base, chunk)].astype(F32)
            nxt = a_ref[pl.ds(base, chunk)].astype(F32)
            window[:, channels : 2 * channels] = x
            for j in range(slabs):
                cut = slice(j * lanes, (j + 1) * lanes)
                wide[j, pl.ds(7, chunk, stride=pitch)] = prev[:, cut]
                wide[j, pl.ds(pitch, chunk, stride=pitch)] = nxt[:, cut]
                for p in range(chunk):
                    wide[j, pl.ds(p * pitch + 8, frames)] = xf[p * frames : (p + 1) * frames, cut]
            for p in range(chunk):
                for j in range(slabs):
                    for offset, to in ((7, 0), (9, 2)):
                        window[
                            p * frames : (p + 1) * frames,
                            to * channels + j * lanes : to * channels + (j + 1) * lanes,
                        ] = wide[j, pl.ds(p * pitch + offset, frames)].astype(BF16)

        def multiply(t):
            window = windows[t % 2]
            totals[t % 2][...] = jnp.dot(window[...], w_ref[...], preferred_element_type=F32)

        def finish(t, sums):
            x = s_ref[pl.ds(base_of(t), chunk)].reshape(count, channels).astype(F32)
            rounded = (x + totals[t % 2][...]).astype(BF16)
            outs[t // per_part][pl.ds(t % per_part * chunk, chunk)] = rounded.reshape(
                chunk, frames, channels
            )
            kept = rounded.astype(F32).reshape(count // 8, 8, channels)
            return sums[0] + jnp.sum(kept, axis=0), sums[1] + jnp.sum(kept * kept, axis=0)

        sums = (jnp.zeros((8, channels), F32),) * 2
        prepare(0)
        for t in range(steps + 1):
            if t < steps:
                multiply(t)
            if t + 1 < steps:
                prepare(t + 1)
            if t > 0:
                sums = finish(t - 1, sums)
        spread = [
            jnp.dot(
                value,
                group_lanes(channels, k * GROUPS),
                precision=lax.Precision.HIGHEST,
                preferred_element_type=F32,
            )
            for k, value in enumerate(sums)
        ]
        row = jnp.sum(spread[0] + spread[1], axis=0, keepdims=True)
        stats_ref[...] = jnp.broadcast_to(row, (8, 128))

    vmem = pl.BlockSpec(memory_space=pltpu.VMEM)
    size = pixels * frames * channels
    res = pl.pallas_call(
        kernel,
        in_specs=[pl.BlockSpec(memory_space=pltpu.SMEM)] + [vmem] * 4,
        out_specs=[vmem] * (parts + 1),
        out_shape=[jax.ShapeDtypeStruct((quarter, frames, channels), BF16)] * parts
        + [jax.ShapeDtypeStruct((8, 128), F32)],
        scratch_shapes=[pltpu.VMEM((slabs, chunk * pitch + 8, lanes), F32)] * 2
        + [pltpu.VMEM((count, 3 * channels), BF16)] * 2
        + [pltpu.VMEM((count, channels), F32)] * 2,
        compiler_params=params(),
        cost_estimate=cost(2 * size * channels * 3, 4 * size),
        name="temporal_conv",
    )(me, spatial, before, after, w_time.reshape(3 * channels, channels))
    return res[:parts], res[parts]


def attention(blocks, stats, gain, bias, w_qkv, w_out, cell_count, first, pixels):
    parts = len(blocks)
    frames, channels = blocks[0].shape[1:]
    length = parts * frames
    group = 8
    head = channels // HEADS
    half = channels // 2
    per_half = HEADS // 2
    factor = math.log2(math.e) / math.sqrt(head)
    batch = 4

    def kernel(*refs):
        ins, refs = refs[:parts], refs[parts:]
        stats_ref, gain_ref, bias_ref, qkv_ref, out_w_ref = refs[:5]
        outs, refs = refs[5 : 5 + parts], refs[5 + parts :]
        normed, projected, contexts, affine = refs[:2], refs[2:4], refs[4], refs[5]
        total = jnp.sum(stats_ref[...], axis=0)
        sums, squares = [
            lax.dot_general(
                total,
                group_lanes(channels, k * GROUPS),
                (((1,), (1,)), ((), ())),
                precision=lax.Precision.HIGHEST,
                preferred_element_type=F32,
            )[0:1]
            for k in range(2)
        ]
        mean = sums / cell_count
        var = jnp.maximum(squares / cell_count - mean * mean, 0.0)
        scale = 0.5 * lax.rsqrt(var + 1e-05) * gain_ref[...]
        affine[0:8] = jnp.broadcast_to(scale, (8, channels))
        affine[8:16] = jnp.broadcast_to(0.5 * bias_ref[...] - mean * scale, (8, channels))
        lane = lax.broadcasted_iota(jnp.int32, (length, channels), 1)
        halves = [(lane // half) == i for i in range(2)]
        heads = [((lane // head) % per_half) == i for i in range(per_half)]

        def normalize(slot, pixel, g):
            x = jnp.concatenate([ref[pixel + g] for ref in ins], axis=0).astype(F32)
            x = x.reshape(length // 8, 8, channels)
            u = (x * affine[0:8][None] + affine[8:16][None]).reshape(length, channels)
            normed[slot][g * length : (g + 1) * length] = (u + u * jnp.tanh(u)).astype(BF16)

        def project(slot, b):
            rows = slice(b * batch * length, (b + 1) * batch * length)
            projected[slot][rows] = jnp.dot(
                normed[slot][rows], qkv_ref[...], preferred_element_type=F32
            ).astype(BF16)

        zero = jnp.zeros((length, channels), BF16)

        def score(slot, g):
            rows = slice(g * length, (g + 1) * length)
            q = projected[slot][rows, :channels]
            k = projected[slot][rows, channels : 2 * channels]
            qm = jnp.concatenate([jnp.where(m, q, zero) for m in halves], axis=0)
            km = jnp.concatenate([jnp.where(m, k, zero) for m in heads], axis=0)
            return lax.dot_general(
                km, qm, (((1,), (1,)), ((), ())), preferred_element_type=F32
            ).reshape(per_half, length, 2 * length)

        def soften(scores):
            top = jnp.max(scores, axis=1, keepdims=True)
            e = jnp.exp2((scores - top) * factor)
            weights = (e * (1.0 / jnp.sum(e, axis=1, keepdims=True))).astype(BF16)
            return weights.reshape(per_half * length, 2 * length)

        def mix(slot, g, weights):
            rows = slice(g * length, (g + 1) * length)
            val = projected[slot][rows, 2 * channels :]
            vm = jnp.concatenate([jnp.where(m, val, zero) for m in heads], axis=0)
            mixed = lax.dot_general(
                weights, vm, (((0,), (0,)), ((), ())), preferred_element_type=F32
            )
            contexts[rows] = jnp.concatenate(
                [mixed[:length, :half], mixed[length:, half:]], axis=1
            ).astype(BF16)

        def finish(slot, pixel, b):
            rows = slice(b * batch * length, (b + 1) * batch * length)
            result = normed[slot][rows].astype(F32) + jnp.dot(
                contexts[rows], out_w_ref[...], preferred_element_type=F32
            )
            result = result.astype(BF16).reshape(batch, parts, frames, channels)
            for d in range(parts):
                outs[d][pl.ds(pixel - first + b * batch, batch)] = result[:, d]

        def work(slot, pixel, ahead):
            scores, weights = {}, {}
            for t in range(group + 2):
                if t < group:
                    scores[t] = score(slot, t)
                    normalize(1 - slot, ahead, t)
                    if (t + 1) % batch == 0:
                        project(1 - slot, t // batch)
                if 0 <= t - 1 < group:
                    weights[t - 1] = soften(scores.pop(t - 1))
                if 0 <= t - 2 < group:
                    mix(slot, t - 2, weights.pop(t - 2))
                    if (t - 1) % batch == 0:
                        finish(slot, pixel, (t - 2) // batch)

        for g in range(group):
            normalize(0, first, g)
        for b in range(group // batch):
            project(0, b)

        def body(i, carry):
            pixel = first + i * 2 * group
            work(0, pixel, pixel + group)
            ahead = jnp.minimum(pixel + 2 * group, first + pixels - group)
            work(1, pixel + group, ahead)
            return carry

        lax.fori_loop(0, pixels // (2 * group), body, 0)

    rest = (stats, gain, bias, w_qkv, w_out)
    vmem = pl.BlockSpec(memory_space=pltpu.VMEM)
    size = parts * pixels * frames * channels
    return pl.pallas_call(
        kernel,
        in_specs=[vmem] * (parts + len(rest)),
        out_specs=[vmem] * parts,
        out_shape=[jax.ShapeDtypeStruct((pixels, frames, channels), BF16)] * parts,
        scratch_shapes=[pltpu.VMEM((group * length, channels), BF16)] * 2
        + [pltpu.VMEM((group * length, 3 * channels), BF16)] * 2
        + [pltpu.VMEM((group * length, channels), BF16), pltpu.VMEM((16, channels), F32)],
        compiler_params=params(),
        cost_estimate=cost(2 * size * channels * 8, 4 * size, size * 3),
        name="attention",
    )(*blocks, *rest)


def from_pixels(me, blocks, moves, shape, result=None):
    frames, rows, cols, channels = shape
    parts = lax.axis_size("tm")
    half_rows = blocks[0].shape[0] // cols
    part_rows = rows // parts
    total = len(blocks) * half_rows
    given = [] if result is None else [result]

    def kernel(me_ref, *refs):
        ins, out_ref, turned, sem = refs[: len(blocks)], refs[-3], refs[-2], refs[-1]
        copies = []
        for n, (d, h) in enumerate(moves):
            base = lax.rem(me_ref[0] + d, parts) * part_rows + h * half_rows
            for r in range(half_rows):
                slot = len(copies)
                turned[slot] = jnp.swapaxes(ins[n][pl.ds(r * cols, cols)], 0, 1)
                copy = pltpu.make_async_copy(turned.at[slot], out_ref.at[:, base + r], sem.at[slot])
                copy.start()
                copies.append(copy)
        for copy in copies:
            copy.wait()

    vmem = pl.BlockSpec(memory_space=pltpu.VMEM)
    anywhere = pl.BlockSpec(memory_space=pl.ANY)
    return pl.pallas_call(
        kernel,
        in_specs=[pl.BlockSpec(memory_space=pltpu.SMEM)]
        + [vmem] * len(blocks)
        + [anywhere] * len(given),
        out_specs=anywhere,
        out_shape=jax.ShapeDtypeStruct(shape, BF16),
        input_output_aliases={1 + len(blocks): 0} if given else {},
        scratch_shapes=[
            pltpu.VMEM((total, frames, cols, channels), BF16),
            pltpu.SemaphoreType.DMA((total,)),
        ],
        compiler_params=params(),
        cost_estimate=cost(0, 4 * total * frames * cols * channels),
        name="from_pixels",
    )(me, *blocks, *given)


def rotate(value, step):
    size = lax.axis_size("tm")
    return lax.ppermute(value, "tm", [(i, (i + step) % size) for i in range(size)])


def per_device(video, w_space, w_time, norm_gain, norm_bias, w_qkv, w_out):
    frames, rows, cols, channels = video.shape
    parts = lax.axis_size("tm")
    me = lax.axis_index("tm").astype(jnp.int32).reshape(1)
    above = shift(video[:, rows - 1], "height", 1)
    below = shift(video[:, 0], "height", -1)
    taps = w_space.reshape(9 * channels, channels)
    first, last = extend_columns(*edge_columns(video), above, below)
    left = shift(last, WIDTH, 1)
    right = shift(first, WIDTH, -1)
    early, late = end_frames(video, above, below, left, right, taps)
    before = shift(late, "tm", 1)
    after = shift(early, "tm", -1)
    spatial = spatial_conv(video, above, below, left, right, taps)
    blocks, stats = temporal_conv(
        me, spatial.reshape(rows * cols, frames, channels), before, after, w_time
    )
    stats = stats + sum(rotate(stats, d) for d in range(1, parts))
    moved = [blocks[0]]
    for d in range(1, parts):
        moved.append(rotate(blocks[d], d))
    stats = stats + lax.ppermute(stats, "width_1", [(0, 1), (1, 0)])
    others = ("height", "width_0")
    count = lax.axis_size(others)
    shared = jnp.broadcast_to(stats[None], (count, *stats.shape))
    stats = lax.all_to_all(shared, others, 0, 0)
    cell_count = float(
        frames * parts * rows * lax.axis_size("height") * cols * lax.axis_size(WIDTH)
        * (channels // GROUPS)
    )
    weights = (norm_gain.reshape(1, -1), norm_bias.reshape(1, -1), w_qkv, w_out)
    share = rows * cols // parts // 2
    own, far = [], []
    for h in range(2):
        results = attention(moved, stats, *weights, cell_count, h * share, share)
        own.append(results[0])
        far.append([])
        for d in range(1, parts):
            far[h].append(rotate(results[d], -d))
    moves = [(0, 0), (0, 1)] + [(d, 0) for d in range(1, parts)]
    result = from_pixels(me, own + far[0], moves, video.shape)
    return from_pixels(me, far[1], [(d, 1) for d in range(1, parts)], video.shape, result)


def solution(mesh):
    torus = Mesh(
        mesh.devices.reshape(mesh.shape["tm"], mesh.shape["height"], 8, 2),
        ("tm", "height", "width_0", "width_1"),
    )
    in_specs = (P("tm", "height", WIDTH, None), P(), P(), P(), P(), P(), P())
    out_specs = P("tm", "height", WIDTH, None)
    return jax.shard_map(
        per_device, mesh=torus, in_specs=in_specs, out_specs=out_specs, check_vma=False
    )
```
